32 devices in a mesh: ctx: 8 (over z, x), head: 4 (over y, core).
Axes of the slice: x: 2, y: 2, z: 4, core: 2. Of those that a mesh axis runs over, the one named last changes fastest.
Arguments:
- mixer_x: bfloat16 [1024, 16384], P('ctx', 'head'), may hold values from -6 to 6
- mixer_bc: bfloat16 [1024, 256], P('ctx'), may hold values from -6 to 6
- dt_raw: float32 [1024, 256], P('ctx', 'head'), may hold values from -4 to 4
- gate_z: bfloat16 [1024, 16384], P('ctx', 'head'), may hold values from -6 to 6
- conv_weight_x: float32 [4, 16384], P(None, 'head'), may hold values from -3 to 3
- conv_bias_x: float32 [16384], P('head'), may hold values from -3 to 3
- conv_weight_bc: float32 [4, 256], replicated, may hold values from -3 to 3
- conv_bias_bc: float32 [256], replicated, may hold values from -3 to 3
- a_log: float32 [256], P('head'), may hold values from -6 to 1
- dt_bias: float32 [256], P('head'), may hold values from -7 to -4
- skip_d: float32 [256], P('head'), may hold values from 0.5 to 2
- d_mixer: bfloat16 [1024, 16384], P('ctx', 'head'), may hold values from -6 to 6
- doc_lengths: int32 [8], replicated, may hold values from 1 to 512, 1024 in all
- att_queries: bfloat16 [1024, 8192], P('ctx', 'head'), may hold values from -144 to 144
- att_keys: bfloat16 [1024, 1024], P('ctx', 'head'), may hold values from -6 to 6
- att_values: bfloat16 [1024, 1024], P('ctx', 'head'), may hold values from -6 to 6
- d_attn: bfloat16 [1024, 8192], P('ctx', 'head'), may hold values from -6 to 6
Outputs:
- grad_mixer_x: bfloat16 [1024, 16384], P('ctx', 'head')
- grad_mixer_bc: bfloat16 [1024, 256], P('ctx')
- grad_dt_raw: float32 [1024, 256], P('ctx', 'head')
- grad_gate_z: bfloat16 [1024, 16384], P('ctx', 'head')
- grad_conv_weight_x: float32 [4, 16384], P(None, 'head')
- grad_conv_bias_x: float32 [16384], P('head')
- grad_conv_weight_bc: float32 [4, 256], replicated
- grad_conv_bias_bc: float32 [256], replicated
- grad_a_log: float32 [256], P('head')
- grad_dt_bias: float32 [256], P('head')
- grad_skip_d: float32 [256], P('head')
- grad_queries: bfloat16 [1024, 8192], P('ctx', 'head')
- grad_keys: bfloat16 [1024, 1024], P('ctx', 'head')
- grad_values: bfloat16 [1024, 1024], P('ctx', 'head')
The draws below stay inside these ranges and needn't reach their ends.
Inputs may be any that keep to these rules, and one draw needn't show every extreme that they name: `doc_lengths`: lengths of 8 documents packed in order, summing to 1024; the longest is exactly 512.
All inputs are finite; a program needn't handle non-finite values.
Results may differ from the reference program's by a relative error of at most 0.0051.
Values may be sent and summed in bfloat16 or wider, within the bound.
No kernel may reach another device: no remote copies, remote signals or barrier semaphores. Data moves between devices by JAX's collectives and lax.ppermute only.
A program may use at most 192 MiB of HBM per device.

```python
import math
import jax
import jax.numpy as jnp
import numpy as np
from jax import lax

MH = 256
MP = 64
NS = 128
KC = 4
AH = 64
KVH = 8
HD = 128
NDOC = 8
TOKENS = 1024


def attention_keys(key):
    base = jax.random.normal(jax.random.fold_in(key, 11), (TOKENS, KVH * HD), jnp.float32)
    return jnp.clip(base, -6.0, 6.0)


def draw_att_keys(key, part):
    return attention_keys(key).astype(jnp.bfloat16)


def draw_att_queries(key, part):
    base = jnp.clip(jax.random.normal(jax.random.fold_in(key, 12), (TOKENS, AH * HD), jnp.float32), -6.0, 6.0)
    return base.astype(jnp.bfloat16)


def level_of(key, shape, cuts, low, top_value):
    def one(axis_at, parts):
        steps = jax.random.uniform(jax.random.fold_in(jax.random.fold_in(key, 6), axis_at), (parts,), jnp.float32, low / len(cuts), top_value / len(cuts))
        return jnp.repeat(jnp.exp(steps), shape[axis_at] // parts).reshape((-1,) + (1,) * (len(shape) - axis_at - 1))

    loudness = one(*cuts[0])
    for cut in cuts[1:]:
        loudness = loudness * one(*cut)
    return loudness


def split_up(count, total, reach, skew):
    portions = [(1 << 20) // math.isqrt(grade ** skew) + 1 for grade in range(2, count + 1)]
    spare, counts = total - reach - (count - 1), [1] * (count - 1)
    while spare > 0:
        movable = [i for i in range(count - 1) if counts[i] < reach]
        mass, remaining = sum([portions[i] for i in movable]), spare
        for i in movable:
            more = min(reach - counts[i], max(1, remaining * portions[i] // mass), spare)
            counts[i] = counts[i] + more
            spare = spare - more
    return np.array([reach] + counts)


def ragged_sizes(rng, number_of, total, limit, skew):
    if number_of == 2:
        one = jax.random.randint(rng, (), max(1, total - limit), min(limit, total - 1) + 1)
        return jnp.stack([one, total - one])
    tallies = jnp.asarray(split_up(number_of, total, limit, skew), jnp.int32)
    pairs = (number_of - 1) // 2
    donor, sink = tallies[1:1 + 2 * pairs:2], tallies[2:2 + 2 * pairs:2]
    room = jnp.minimum(donor - 1, limit - sink)
    passed = jax.random.randint(jax.random.fold_in(rng, 1), (pairs,), 0, 1 << 20) % (room + 1)
    tallies = tallies.at[1:1 + 2 * pairs:2].set(donor - passed).at[2:2 + 2 * pairs:2].set(sink + passed)
    return tallies[jax.random.permutation(jax.random.fold_in(rng, 2), number_of)]


def noise(own_key, dims, spread, limit, shards=(), kind=jnp.bfloat16):
    drawn = spread * jax.random.normal(own_key, dims, jnp.float32)
    if shards:
        drawn = drawn * level_of(own_key, dims, shards, -0.22, 0.18)
    return jnp.clip(drawn, -limit, limit).astype(kind)


def setup_inputs(seed: int = 0) -> dict:
    streams_of = jax.random.split(jax.random.key(seed), 18)
    mixer_x = noise(streams_of[0], (TOKENS, MH * MP), 1.0, 6.0, ((0, 8), (1, 4)))
    mixer_bc = noise(streams_of[1], (TOKENS, 2 * NS), 1.0, 6.0, ((0, 8),))
    dt_raw = noise(streams_of[2], (TOKENS, MH), 1.0, 4.0, ((0, 8), (1, 4)), jnp.float32)
    gate_z = noise(streams_of[3], (TOKENS, MH * MP), 1.0, 6.0, ((0, 8), (1, 4)))
    conv_weight_x = noise(streams_of[4], (KC, MH * MP), KC ** -0.5, 3.0, ((1, 4),), jnp.float32)
    conv_bias_x = noise(streams_of[5], (MH * MP,), 0.5, 3.0, ((0, 4),), jnp.float32)
    conv_weight_bc = noise(streams_of[6], (KC, 2 * NS), KC ** -0.5, 3.0, (), jnp.float32)
    conv_bias_bc = noise(streams_of[7], (2 * NS,), 0.5, 3.0, (), jnp.float32)
    a_log = jnp.clip(-6.0 + 7.0 * jax.random.uniform(streams_of[8], (MH,), jnp.float32) ** level_of(streams_of[8], (MH,), ((0, 4),), -0.2, 0.2), -6.0, 1.0)
    dt_bias = jnp.clip(-7.0 + 3.0 * jax.random.uniform(streams_of[9], (MH,), jnp.float32) ** level_of(streams_of[9], (MH,), ((0, 4),), -0.2, 0.2), -7.0, -4.0)
    skip_d = jnp.clip(0.5 + 1.5 * jax.random.uniform(streams_of[10], (MH,), jnp.float32) ** level_of(streams_of[10], (MH,), ((0, 4),), -0.2, 0.2), 0.5, 2.0)
    d_mixer = noise(streams_of[11], (TOKENS, MH * MP), 1.0, 6.0, ((0, 8), (1, 4)))
    doc_lengths = ragged_sizes(streams_of[12], NDOC, TOKENS, TOKENS // 2, 2).astype(jnp.int32)
    att_queries = draw_att_queries(jax.random.fold_in(streams_of[17], 71), 0)
    att_keys = draw_att_keys(jax.random.fold_in(streams_of[17], 71), 0)
    att_values = noise(streams_of[15], (TOKENS, KVH * HD), 1.0, 6.0, ((0, 8), (1, 4)))
    d_attn = noise(streams_of[16], (TOKENS, AH * HD), 1.0, 6.0, ((0, 8), (1, 4)))
    return {"mixer_x": mixer_x, "mixer_bc": mixer_bc, "dt_raw": dt_raw, "gate_z": gate_z, "conv_weight_x": conv_weight_x, "conv_bias_x": conv_bias_x, "conv_weight_bc": conv_weight_bc, "conv_bias_bc": conv_bias_bc, "a_log": a_log, "dt_bias": dt_bias, "skip_d": skip_d, "d_mixer": d_mixer, "doc_lengths": doc_lengths, "att_queries": att_queries, "att_keys": att_keys, "att_values": att_values, "d_attn": d_attn}


FILL_SCORE = -1e+30
HIGHEST = lax.Precision.HIGHEST

def doc_index(positions, doc_lengths):
    ends = jnp.cumsum(doc_lengths).astype(jnp.int32)
    return lax.optimization_barrier(jnp.sum((ends[None, :] <= positions[:, None]).astype(jnp.int32), axis=1)).astype(jnp.int32)

def conv_silu(padded, weight, bias_row, seg_pad, row_count):
    seg_now = seg_pad[KC - 1:]
    summed = jnp.broadcast_to(bias_row[None, :], (row_count, bias_row.shape[0]))
    for tap_index in range(KC):
        offset = KC - 1 - tap_index
        lagged = padded[offset:offset + row_count]
        same_doc = (seg_pad[offset:offset + row_count] == seg_now).astype(jnp.float32)
        summed = summed + weight[tap_index][None, :] * lagged * same_doc[:, None]
    return jax.nn.silu(summed)

def ssd_scan(inputs_x, steps_dt, decay_log, b_in, c_out, seg_now, seg_start):
    row_count, head_count, head_width = inputs_x.shape
    block_rows = min(128, row_count)
    block_count = row_count // block_rows

    def by_block(array):
        return array.reshape((block_count, block_rows) + array.shape[1:])
    causal = jnp.arange(block_rows)[:, None] >= jnp.arange(block_rows)[None, :]

    def advance(carried, pieces):
        running, seg_before = carried
        xblock, dtblock, ablock, bblock, cblock, sblock = pieces
        cum_log = jnp.cumsum(ablock, axis=0)
        heads_cum = cum_log.T
        allowed = causal & (sblock[:, None] == sblock[None, :])
        log_gaps = heads_cum[:, :, None] - heads_cum[:, None, :]
        within = jnp.exp(jnp.where(allowed[None], log_gaps, FILL_SCORE))
        c_dot_b = jnp.dot(cblock, bblock.T, precision=HIGHEST)
        weighted = dtblock[:, :, None] * xblock
        within_sum = jnp.einsum('hts,shp->thp', within * c_dot_b[None], weighted, precision=HIGHEST)
        entry_block = jnp.exp(cum_log) * (sblock == seg_before).astype(jnp.float32)[:, None]
        from_state = jnp.einsum('tn,hpn->thp', cblock, running, precision=HIGHEST) * entry_block[:, :, None]
        last_log = cum_log[-1]
        seg_last = sblock[-1]
        leaving = jnp.exp(last_log[None, :] - cum_log) * (sblock == seg_last).astype(jnp.float32)[:, None]
        kept_share = jnp.exp(last_log) * (seg_last == seg_before).astype(jnp.float32)
        added_state = jnp.einsum('shp,sn->hpn', leaving[:, :, None] * weighted, bblock, precision=HIGHEST)
        return ((running * kept_share[:, None, None] + added_state, seg_last), within_sum + from_state)
    start_state = (jnp.zeros((head_count, head_width, b_in.shape[1]), jnp.float32), seg_start)
    pieces = (by_block(inputs_x), by_block(steps_dt), by_block(decay_log), by_block(b_in), by_block(c_out), by_block(seg_now))
    (last_state, seg_final), outputs = lax.scan(advance, start_state, pieces)
    return (outputs.reshape(row_count, head_count, head_width), last_state)

def mixer_front(raw_x, raw_bc, margin, dt_raw, weight_x, bias_x, weight_bc, bias_bc, a_log, dt_bias, skip_d, seg_pad, seg_start):
    row_count, channels = raw_x.shape
    seg_now = seg_pad[KC - 1:]
    conv_x = conv_silu(jnp.concatenate([margin[:, :channels], raw_x], axis=0), weight_x, bias_x, seg_pad, row_count)
    conv_bc = conv_silu(jnp.concatenate([margin[:, channels:], raw_bc], axis=0), weight_bc, bias_bc, seg_pad, row_count)
    b_in = conv_bc[:, :NS]
    c_out = conv_bc[:, NS:]
    steps_dt = jax.nn.softplus(dt_raw + dt_bias[None, :])
    decay_log = -steps_dt * jnp.exp(a_log)[None, :]
    inputs_x = conv_x.reshape(row_count, channels // MP, MP)
    within_sum, last_state = ssd_scan(inputs_x, steps_dt, decay_log, b_in, c_out, seg_now, seg_start)
    ungated = within_sum + skip_d[None, :, None] * inputs_x
    entry_decay = jnp.exp(jnp.cumsum(decay_log, axis=0)) * (seg_now == seg_start).astype(jnp.float32)[:, None]
    return (ungated, last_state, entry_decay[-1], c_out, entry_decay)

def mixer_gate(ungated, c_out, entry_decay, gate_value, incoming):
    from_before = jnp.einsum('tn,hpn->thp', c_out, incoming, precision=HIGHEST) * entry_decay[:, :, None]
    summed = (ungated + from_before).reshape(ungated.shape[0], -1)
    return summed * jax.nn.silu(gate_value)

def attention_reference(att_queries, att_keys, att_values, d_attn, doc_lengths):
    token_count = att_queries.shape[0]
    inv_root = 1.0 / math.sqrt(HD)
    group_size = AH // KVH
    positions = jnp.arange(token_count, dtype=jnp.int32)
    seg_all = doc_index(positions, doc_lengths)
    allowed = (positions[None, :] <= positions[:, None]) & (seg_all[None, :] == seg_all[:, None])
    query_heads = att_queries.reshape(token_count, AH, HD).transpose(1, 0, 2)
    grad_heads = d_attn.reshape(token_count, AH, HD).transpose(1, 0, 2)
    key_heads = att_keys.reshape(token_count, KVH, HD).transpose(1, 0, 2)
    value_heads = att_values.reshape(token_count, KVH, HD).transpose(1, 0, 2)

    def one_head(head_index):
        shared = head_index // group_size
        query_rows = query_heads[head_index]
        grad_rows = grad_heads[head_index]
        key_rows = key_heads[shared]
        value_rows = value_heads[shared]
        scores = jnp.dot(query_rows, key_rows.T, preferred_element_type=jnp.float32) * inv_root
        scores = jnp.where(allowed, scores, FILL_SCORE)
        row_top = lax.optimization_barrier(jnp.max(scores, axis=-1))
        weights = jnp.exp(scores - row_top[:, None])
        softmax = weights / lax.optimization_barrier(jnp.sum(weights, axis=-1))[:, None]
        attended = jnp.dot(softmax, value_rows.astype(jnp.float32), precision=HIGHEST)
        row_delta = lax.optimization_barrier(jnp.sum(grad_rows.astype(jnp.float32) * attended, axis=-1))
        softmax_low = softmax.astype(jnp.bfloat16)
        grad_value = jnp.dot(softmax_low.T, grad_rows, preferred_element_type=jnp.float32)
        grad_prob = jnp.dot(grad_rows, value_rows.T, preferred_element_type=jnp.float32)
        grad_score = (softmax * (grad_prob - row_delta[:, None])).astype(jnp.bfloat16)
        grad_query = jnp.dot(grad_score, key_rows, preferred_element_type=jnp.float32) * inv_root
        grad_key = jnp.dot(grad_score.T, query_rows, preferred_element_type=jnp.float32) * inv_root
        return (grad_query, grad_key, grad_value)
    grad_q, grad_k, grad_v = lax.map(one_head, jnp.arange(AH, dtype=jnp.int32))
    grad_q = grad_q.transpose(1, 0, 2).reshape(token_count, AH * HD).astype(jnp.bfloat16)
    grad_k = grad_k.reshape(KVH, group_size, token_count, HD).sum(axis=1)
    grad_v = grad_v.reshape(KVH, group_size, token_count, HD).sum(axis=1)
    grad_k = grad_k.transpose(1, 0, 2).reshape(token_count, KVH * HD).astype(jnp.bfloat16)
    grad_v = grad_v.transpose(1, 0, 2).reshape(token_count, KVH * HD).astype(jnp.bfloat16)
    return (grad_q, grad_k, grad_v)

def reference(mixer_x, mixer_bc, dt_raw, gate_z, conv_weight_x, conv_bias_x, conv_weight_bc, conv_bias_bc, a_log, dt_bias, skip_d, d_mixer, doc_lengths, att_queries, att_keys, att_values, d_attn):
    token_count, channels = mixer_x.shape
    positions = jnp.arange(-(KC - 1), token_count, dtype=jnp.int32)
    seg_pad = doc_index(positions, doc_lengths)
    seg_start = seg_pad[KC - 2]
    margin = jnp.zeros((KC - 1, channels + 2 * NS), jnp.float32)
    no_state = jnp.zeros((channels // MP, MP, NS), jnp.float32)

    def whole(raw_x, raw_bc, raw_dt, gate_value, weight_x, bias_x, weight_bc, bias_bc, log_rate, step_bias, skip_gain):
        ungated, last_state, decay_total, c_out, entry_decay = mixer_front(raw_x, raw_bc, margin, raw_dt, weight_x, bias_x, weight_bc, bias_bc, log_rate, step_bias, skip_gain, seg_pad, seg_start)
        return mixer_gate(ungated, c_out, entry_decay, gate_value, no_state)
    mixed, pullback = jax.vjp(whole, mixer_x.astype(jnp.float32), mixer_bc.astype(jnp.float32), dt_raw, gate_z.astype(jnp.float32), conv_weight_x, conv_bias_x, conv_weight_bc, conv_bias_bc, a_log, dt_bias, skip_d)
    grad_parts = pullback(d_mixer.astype(jnp.float32))
    grad_q, grad_k, grad_v = attention_reference(att_queries, att_keys, att_values, d_attn, doc_lengths)
    return (grad_parts[0].astype(jnp.bfloat16), grad_parts[1].astype(jnp.bfloat16), grad_parts[2], grad_parts[3].astype(jnp.bfloat16), grad_parts[4], grad_parts[5], grad_parts[6], grad_parts[7], grad_parts[8], grad_parts[9], grad_parts[10], grad_q, grad_k, grad_v)
```

```python
import math

import jax
import jax.numpy as jnp
from jax import lax
from jax.experimental import pallas as pl
from jax.experimental.pallas import tpu as pltpu
from jax.sharding import PartitionSpec as P


MP = 64
KC = 4
AH = 64
KVH = 8
HD = 128
RB = 128
FILL = -1e30
F32 = jnp.float32
BF16 = jnp.bfloat16
HIGHEST = lax.Precision.HIGHEST


def params(limit=56):
    return pltpu.CompilerParams(vmem_limit_bytes=limit * 1024 * 1024)


def shifted(value, axis, steps):
    count = lax.axis_size(axis)
    initial, last = (max(0, -steps), min(count, count - steps))
    return lax.ppermute(value, axis, [(source, source + steps) for source in range(initial, last)])


def crossed(value, axis, mask):
    count = lax.axis_size(axis)
    return lax.ppermute(value, axis, [(source, source ^ mask) for source in range(count)])


def dot(a, b, dims=((1,), (0,)), precision=None):
    return lax.dot_general(a, b, (dims, ((), ())), precision=precision, preferred_element_type=F32)


NN = ((1,), (0,))
NT = ((1,), (1,))
TN = ((0,), (0,))


def iota(shape, dim):
    return lax.broadcasted_iota(jnp.int32, shape, dim)


def doc_start(doc_ref, pos):
    end = jnp.int32(0)
    start = jnp.zeros_like(pos)
    for j in range(doc_ref.shape[0]):
        end = end + doc_ref[j]
        start = jnp.where(pos >= end, end, start)
    return start


def smem():
    return pl.BlockSpec(memory_space=pltpu.SMEM)


def vmem():
    return pl.BlockSpec(memory_space=pltpu.VMEM)


def attention_kernel(reach, idx_ref, doc_ref, q_ref, do_ref, *rest):
    nb = reach + 1
    kv_refs = rest[:nb]
    dq_ref = rest[nb]
    out_refs = rest[nb + 1 : 2 * nb + 1]
    k_ref, v_ref, kt_ref, mask_ref, qc_ref, dc_ref, p_ref, g_ref = rest[2 * nb + 1 :]
    group = AH // KVH
    kv_count = q_ref.shape[1] // (group * HD)
    inv_root = 1.0 / math.sqrt(HD)
    keys = nb * RB
    first = idx_ref[0] * RB
    q_pos = first + iota((8, RB), 1)
    q_start = doc_start(doc_ref, q_pos)[:1]
    k_pos = first - reach * RB + iota((keys, RB), 0)
    allowed = (k_pos <= q_pos[:1]) & (k_pos >= q_start)
    mask_ref[...] = jnp.where(allowed, 0.0, FILL)
    for kv in range(kv_count):
        for b in range(nb):
            k_ref[pl.ds(b * RB, RB), :] = kv_refs[b][:, pl.ds(kv * HD, HD)]
            v_ref[pl.ds(b * RB, RB), :] = kv_refs[b][:, pl.ds((kv_count + kv) * HD, HD)]
        kt_ref[...] = k_ref[...].astype(F32).T.astype(BF16)

        def head(h, carry):
            lanes = pl.ds(pl.multiple_of((kv * group + h) * HD, HD), HD)
            rows = pl.ds(pl.multiple_of(h * RB, RB), RB)
            q = q_ref[:, lanes]
            do = do_ref[:, lanes]
            qc_ref[rows, :] = q
            dc_ref[rows, :] = do
            scores = dot(k_ref[...], q, NT) * inv_root + mask_ref[...]
            top = jnp.max(scores, axis=0, keepdims=True)
            weights = jnp.exp(scores - top)
            softmax = weights * (1.0 / jnp.sum(weights, axis=0, keepdims=True))
            grad_prob = dot(v_ref[...], do, NT)
            delta = jnp.sum(softmax * grad_prob, axis=0, keepdims=True)
            grad_score = (softmax * (grad_prob - delta)).astype(BF16)
            p_ref[:, rows] = softmax.astype(BF16)
            g_ref[:, rows] = grad_score
            grad_q = dot(kt_ref[...], grad_score, NN) * inv_root
            dq_ref[:, lanes] = grad_q.T.astype(BF16)
            return carry

        lax.fori_loop(0, group, head, 0)
        grad_k = dot(g_ref[...], qc_ref[...], NN) * inv_root
        grad_v = dot(p_ref[...], dc_ref[...], NN)
        for b in range(nb):
            kind = out_refs[b].dtype
            rows = slice(b * RB, (b + 1) * RB)
            out_refs[b][:, pl.ds(kv * HD, HD)] = grad_k[rows].astype(kind)
            out_refs[b][:, pl.ds((kv_count + kv) * HD, HD)] = grad_v[rows].astype(kind)


def attention_call(idx, doc, queries, grads, blocks):
    nb = len(blocks)
    keys = nb * RB
    group = AH // KVH
    outs = [jax.ShapeDtypeStruct(queries.shape, BF16)]
    outs += [jax.ShapeDtypeStruct(blocks[0].shape, BF16)] * (nb - 1)
    outs += [jax.ShapeDtypeStruct(blocks[0].shape, F32)]
    return pl.pallas_call(
        lambda *refs: attention_kernel(nb - 1, *refs),
        out_shape=outs,
        in_specs=[smem(), smem()] + [vmem()] * (2 + nb),
        out_specs=[vmem()] * (1 + nb),
        scratch_shapes=[
            pltpu.VMEM((keys, HD), BF16),
            pltpu.VMEM((keys, HD), BF16),
            pltpu.VMEM((HD, keys), BF16),
            pltpu.VMEM((keys, RB), F32),
            pltpu.VMEM((group * RB, HD), BF16),
            pltpu.VMEM((group * RB, HD), BF16),
            pltpu.VMEM((keys, group * RB), BF16),
            pltpu.VMEM((keys, group * RB), BF16),
        ],
        compiler_params=params(),
        name="attention",
    )(idx, doc, queries, grads, *blocks)


def pack_kernel(n, idx_ref, x_ref, z_ref, d_ref, *outs):
    width = x_ref.shape[1] // n
    me = idx_ref[0]
    for m in range(n):
        lanes = pl.ds(pl.multiple_of((me ^ m) * width, 128), width)
        z = z_ref[:, lanes].astype(F32)
        grad = d_ref[:, lanes].astype(F32) * z * jax.nn.sigmoid(z)
        outs[m][:, :width] = x_ref[:, lanes]
        outs[m][:, width:] = grad.astype(BF16)


def pack_call(n, idx, mixer_x, gate_z, d_mixer):
    rows, channels = mixer_x.shape
    width = channels // n
    return pl.pallas_call(
        lambda *refs: pack_kernel(n, *refs),
        out_shape=[jax.ShapeDtypeStruct((rows, 2 * width), BF16)] * n,
        in_specs=[smem()] + [vmem()] * 3,
        out_specs=[vmem()] * n,
        compiler_params=params(),
        name="pack",
    )(idx, mixer_x, gate_z, d_mixer)


def unpack_kernel(n, hp, idx_ref, z_ref, d_ref, *refs):
    big = refs[:n]
    small = refs[n : 2 * n]
    gx_ref, gz_ref, gw_ref, ddt_ref, hv_ref = refs[2 * n :]
    width = z_ref.shape[1] // n
    pairs = width // 128
    me = idx_ref[0]
    for m in range(n):
        source = me ^ m
        lanes = pl.ds(pl.multiple_of(source * width, 128), width)
        gx_ref[:, lanes] = big[m][:, :width]
        z = z_ref[:, lanes].astype(F32)
        sig = jax.nn.sigmoid(z)
        y = big[m][:, width:].astype(F32)
        gz_ref[:, lanes] = (d_ref[:, lanes].astype(F32) * y * (sig * (1.0 + z * (1.0 - sig)))).astype(BF16)
        ddt_ref[pl.ds(pl.multiple_of(source * hp, 8), hp), :] = small[m][:hp, :]
        for p in range(pairs):
            part = pl.ds(pl.multiple_of(source * width + p * 128, 128), 128)
            gw_ref[:, part] = small[m][hp + 8 * p : hp + 8 * p + 8, :]
        at = hp + 8 * pairs + 16
        hv_ref[pl.ds(pl.multiple_of(source * hp, 8), hp), :128] = small[m][at : at + hp, :]
        hv_ref[pl.ds(pl.multiple_of(source * hp, 8), hp), 128:] = small[m][at + hp : at + 2 * hp, :]


def unpack_call(n, hp, idx, gate_z, d_mixer, big, small):
    rows, channels = gate_z.shape
    return pl.pallas_call(
        lambda *refs: unpack_kernel(n, hp, *refs),
        out_shape=[
            jax.ShapeDtypeStruct((rows, channels), BF16),
            jax.ShapeDtypeStruct((rows, channels), BF16),
            jax.ShapeDtypeStruct((8, channels), F32),
            jax.ShapeDtypeStruct((n * hp, 128), F32),
            jax.ShapeDtypeStruct((n * hp, 256), F32),
        ],
        in_specs=[smem()] + [vmem()] * (2 + 2 * n),
        out_specs=[vmem()] * 5,
        compiler_params=params(),
        name="unpack",
    )(idx, gate_z, d_mixer, *big, *small)


def by_sublane(value):
    return jnp.sum(value.reshape(value.shape[0] // 8, 8, value.shape[1]), axis=0)


def mixer_kernel(n, heads, hp, idx_ref, doc_ref, *refs):
    width = heads * MP
    pairs = width // 128
    wide = 2 - pairs % 2
    xd_in = refs[:n]
    bc_in = refs[n : 2 * n]
    dt_in = refs[2 * n : 3 * n]
    wx_ref, bx_ref, wbc_ref, bbc_ref, par_ref = refs[3 * n : 3 * n + 5]
    at = 3 * n + 5
    big_out = refs[at : at + n]
    bc_out = refs[at + n : at + 2 * n]
    small_out = refs[at + 2 * n : at + 3 * n]
    (
        xd_ref,
        od_ref,
        raw_ref,
        og_ref,
        off_ref,
        xs_ref,
        gp_ref,
        bb_ref,
        cc_ref,
        bt_ref,
        ct_ref,
        cb_ref,
        bias_ref,
        dcb_ref,
        db_ref,
        dc_ref,
        step_ref,
        cum_ref,
        sg_ref,
        z1_ref,
        z2_ref,
        sin_ref,
        yn_ref,
        dwi_ref,
        lv_ref,
        st_ref,
        xc_ref,
        ds_ref,
        ed_ref,
        k_ref,
        acc_ref,
    ) = refs[at + 3 * n :]
    me = idx_ref[0]
    tokens = n * RB
    lane = iota((RB, 128), 1)
    sub = iota((RB, 128), 0)
    low = lane < MP
    zero8 = jnp.zeros((8, 128), F32)

    def rows_of(c, extra=0):
        return pl.ds(pl.multiple_of(c * RB, RB), RB + extra)

    upper = (sub <= lane).astype(F32)
    e_log = jnp.exp(par_ref[0])
    for m in range(n):
        source = me ^ m
        rows = rows_of(source)
        xd_ref[rows, :] = xd_in[m][...]
        raw_ref[pl.ds(pl.multiple_of(source * RB + 8, 8), RB), :] = bc_in[m][...].astype(F32)
        logit = dt_in[m][...] + par_ref[1]
        tail = jnp.exp(-jnp.abs(logit))
        step = jnp.maximum(logit, 0.0) + jnp.log1p(tail)
        step_ref[source] = step
        sg_ref[source] = jax.nn.sigmoid(logit)
        cum_ref[source] = dot(-step * e_log, upper, NN, HIGHEST)
        z1_ref[source] = jnp.zeros((hp, 128), F32)
        z2_ref[source] = jnp.zeros((hp, 128), F32)
        dcb_ref[source] = jnp.zeros((RB, RB), F32)
        db_ref[source] = jnp.zeros((RB, 128), F32)
        dc_ref[source] = jnp.zeros((RB, 128), F32)
    raw_ref[:8, :] = jnp.zeros((8, 256), F32)
    for u in range(wide):
        xs_ref[u, :8, :] = zero8
        for j in range(KC - 1):
            gp_ref[u, j, tokens:, :] = zero8
    off_ref[tokens:, :] = jnp.zeros((8, 128), jnp.int32)

    def conv(c, src_ref, lanes, weight, bias):
        off = off_ref[rows_of(c), :]
        window = src_ref[rows_of(c, 8), lanes]
        lags = [window[8:]]
        for j in range(1, KC):
            lags.append(jnp.where(off >= j, window[8 - j : 8 + RB - j], 0.0))
        pre = bias
        for j in range(KC):
            pre = pre + weight[j : j + 1] * lags[j]
        return pre, lags

    def conv_back(c, grad, src_ref, lanes, weight, u):
        off = off_ref[rows_of(c), :]
        window = src_ref[rows_of(c, 8), lanes]
        back = weight[0:1] * grad
        sums = [by_sublane(grad * window[8:])]
        for j in range(1, KC):
            held_back = jnp.where(off >= j, grad, 0.0)
            sums.append(by_sublane(held_back * window[8 - j : 8 + RB - j]))
            gp_ref[u, j - 1, rows_of(c), :] = held_back
            back = back + weight[j : j + 1] * gp_ref[u, j - 1, rows_of(c, 8), :][j : j + RB]
        sums.append(by_sublane(grad))
        return back, sums

    def silu_parts(pre):
        sig = jax.nn.sigmoid(pre)
        return pre * sig, sig * (1.0 + pre * (1.0 - sig))

    wbc = wbc_ref[...]
    bbc = bbc_ref[...]

    def prepare(c, carry):
        pos = c * RB + sub
        off = pos - doc_start(doc_ref, pos)
        off_ref[rows_of(c), :] = off
        allowed = (lane <= sub) & (sub - lane <= off)
        bias_ref[c] = jnp.where(allowed, 0.0, FILL)
        pre_b, unused = conv(c, raw_ref, slice(0, 128), wbc[:, :128], bbc[:, :128])
        pre_c, unused = conv(c, raw_ref, slice(128, 256), wbc[:, 128:], bbc[:, 128:])
        b_in = silu_parts(pre_b)[0]
        c_out = silu_parts(pre_c)[0]
        b_low, c_low = b_in.astype(BF16), c_out.astype(BF16)
        bb_ref[rows_of(c), :] = b_low
        cc_ref[rows_of(c), :] = c_low
        bt_ref[c] = b_in.T.astype(BF16)
        ct_ref[c] = c_out.T.astype(BF16)
        cb_ref[c] = dot(c_low, b_low, NT)
        return carry

    lax.fori_loop(0, n, prepare, 0)

    def streams(block, carry):
        ids = [block * wide + u for u in range(wide)]
        each = range(wide)
        lanes = [pl.ds(pl.multiple_of(p * 128, 128), 128) for p in ids]
        lanes_d = [pl.ds(pl.multiple_of(width + p * 128, 128), 128) for p in ids]
        held = [pl.ds(pl.multiple_of(me * width + p * 128, 128), 128) for p in ids]
        weight = [wx_ref[:, h] for h in held]
        bias = [bx_ref[:, h] for h in held]
        skip = [
            jnp.where(low[:1], par_ref[2, pl.ds(2 * p, 1), :], par_ref[2, pl.ds(2 * p + 1, 1), :]) for p in ids
        ]
        pick = [
            jnp.where(iota((hp, 128), 0) == 2 * p + iota((hp, 128), 1) // MP, 1.0, 0.0).astype(BF16) for p in ids
        ]

        def load(c, unused):
            for u in each:
                xs_ref[u, pl.ds(pl.multiple_of(c * RB + 8, 8), RB), :] = xd_ref[rows_of(c), lanes[u]].astype(F32)
            return unused

        lax.fori_loop(0, n, load, 0)

        def forward_one(u, c, state):
            p = ids[u]
            rows = rows_of(c)
            off = off_ref[rows, :]
            pre, _ = conv(c, xs_ref.at[u], slice(None), weight[u], bias[u])
            x, slope = silu_parts(pre)
            xc_ref[u, rows, :] = x
            ds_ref[u, rows, :] = slope
            row0 = cum_ref[c, pl.ds(2 * p, 1), :]
            row1 = cum_ref[c, pl.ds(2 * p + 1, 1), :]
            col0 = jnp.broadcast_to(row0, (128, RB)).T
            col1 = jnp.broadcast_to(row1, (128, RB)).T
            step0 = step_ref[c, pl.ds(2 * p, 1), :]
            step1 = step_ref[c, pl.ds(2 * p + 1, 1), :]
            step = jnp.where(sub < MP, step0, step1).T
            st_ref[u, rows, :] = step
            cum = jnp.where(low, col0, col1)
            mask = bias_ref[c]
            cb = cb_ref[c]
            decay0 = jnp.exp(col0 - row0 + mask)
            decay1 = jnp.exp(col1 - row1 + mask)
            mix0 = (decay0 * cb).astype(BF16)
            mix1 = (decay1 * cb).astype(BF16)
            value = step * x
            grad = xd_ref[rows, lanes_d[u]].astype(F32)
            value_low = value.astype(BF16)
            value_two = jnp.concatenate(
                [jnp.where(low, value, 0.0).astype(BF16), jnp.where(low, 0.0, value).astype(BF16)], axis=0
            )
            grad_two = jnp.concatenate(
                [jnp.where(low, grad, 0.0).astype(BF16), jnp.where(low, 0.0, grad).astype(BF16)], axis=0
            )
            inner = dot(jnp.concatenate([mix0, mix1], axis=1), value_two, NN)
            dwi_ref[u, rows, :] = dot(jnp.concatenate([mix0, mix1], axis=0), grad_two, TN)
            grad_mix = dot(grad_two, value_low, NT)
            added = decay0 * grad_mix[:RB] + decay1 * grad_mix[RB:]
            enter = jnp.where(off > sub, jnp.exp(cum), 0.0)
            last = cum[RB - 1 :]
            off_last = off[RB - 1 :]
            leave = jnp.where(sub >= RB - 1 - off_last, jnp.exp(last - cum), 0.0)
            keep = jnp.where(off_last >= RB, jnp.exp(last), 0.0)
            lv_ref[u, rows, :] = leave
            k_ref[u, c] = jnp.broadcast_to(keep, (8, 128))
            sin_ref[u, c] = state
            state_low = state.astype(BF16)
            total = inner + enter * dot(cc_ref[rows, :], state_low, NN)
            yn_ref[u, rows, :] = total
            od_ref[rows, lanes_d[u]] = (total + skip[u] * x).astype(BF16)
            entered = (enter * grad).astype(BF16)
            ed_ref[u, rows, :] = entered
            new_state = keep * state + dot(bt_ref[c], (leave * value).astype(BF16), NN)
            return new_state, added, dot(entered, state_low, NT)

        def forward(c, states):
            found = [forward_one(u, c, states[u]) for u in each]
            dcb_ref[c] += sum(f[1] for f in found)
            dc_ref[c] += sum(f[2] for f in found)
            return tuple(f[0] for f in found)

        nothing = tuple(jnp.zeros((128, 128), F32) for u in each)
        final = lax.fori_loop(0, n, forward, nothing)
        for u in each:
            sin_ref[u, n] = final[u]
            for j in range(KC + 2):
                acc_ref[u, j] = zero8

        def backward_one(u, c, later):
            rows = rows_of(c)
            later_low = later.astype(BF16)
            leave = lv_ref[u, rows, :]
            x = xc_ref[u, rows, :]
            step = st_ref[u, rows, :]
            grad = xd_ref[rows, lanes_d[u]].astype(F32)
            value = step * x
            grad_value = dwi_ref[u, rows, :] + leave * dot(bb_ref[rows, :], later_low, NN)
            z1 = grad * yn_ref[u, rows, :] - value.astype(BF16).astype(F32) * grad_value
            carried = jnp.sum(later_low.astype(F32) * sin_ref[u, c + 1], axis=0, keepdims=True)
            z1 = jnp.concatenate([z1[: RB - 8], z1[RB - 8 :] + jnp.where(sub[RB - 8 :] == RB - 1, carried, 0.0)], axis=0)
            z1_high = z1.astype(BF16)
            z1_rest = (z1 - z1_high.astype(F32)).astype(BF16)
            rates = dot(pick[u], z1_high, NT) + dot(pick[u], z1_rest, NT)
            steps = dot(pick[u], (x * grad_value).astype(BF16), NT)
            grad_b = dot((leave * value).astype(BF16), later_low, NT)
            grad_x = (step * grad_value + skip[u] * grad) * ds_ref[u, rows, :]
            back, sums = conv_back(c, grad_x, xs_ref.at[u], slice(None), weight[u], u)
            od_ref[rows, lanes[u]] = back.astype(BF16)
            sums.append(by_sublane(grad * x))
            for j in range(KC + 2):
                acc_ref[u, j] += sums[j]
            new_later = k_ref[u, c][:1] * later + dot(ct_ref[c], ed_ref[u, rows, :], NN)
            return new_later, rates, steps, grad_b

        def backward(k, laters):
            c = n - 1 - k
            found = [backward_one(u, c, laters[u]) for u in each]
            z1_ref[c] += sum(f[1] for f in found)
            z2_ref[c] += sum(f[2] for f in found)
            db_ref[c] += sum(f[3] for f in found)
            return tuple(f[0] for f in found)

        lax.fori_loop(0, n, backward, nothing)
        for u in each:
            found = [jnp.sum(acc_ref[u, j], axis=0, keepdims=True) for j in range(KC + 2)]
            found.append(jnp.zeros((8 - KC - 2, 128), F32))
            at_row = pl.multiple_of(hp + 8 * ids[u], 8)
            small_out[0][pl.ds(at_row, 8), :] = jnp.concatenate(found, axis=0)
        return carry

    lax.fori_loop(0, pairs // wide, streams, 0)

    for side in range(2):
        lanes = slice(128 * side, 128 * side + 128)
        weight = wbc[:, lanes]
        bias = bbc[:, lanes]
        for j in range(KC + 1):
            acc_ref[0, j] = zero8

        def finish(k, carry):
            c = n - 1 - k
            rows = rows_of(c)
            mixed = dcb_ref[c].astype(BF16)
            if side == 0:
                grad = db_ref[c] + dot(mixed, cc_ref[rows, :], TN)
            else:
                grad = dc_ref[c] + dot(mixed, bb_ref[rows, :], NN)
            pre, _ = conv(c, raw_ref, lanes, weight, bias)
            back, sums = conv_back(c, grad * silu_parts(pre)[1], raw_ref, lanes, weight, 0)
            og_ref[rows, lanes] = back.astype(BF16)
            for j in range(KC + 1):
                acc_ref[0, j] += sums[j]
            return carry

        lax.fori_loop(0, n, finish, 0)
        found = [jnp.sum(acc_ref[0, j], axis=0, keepdims=True) for j in range(KC + 1)]
        found.append(jnp.zeros((8 - KC - 1, 128), F32))
        first = hp + 8 * pairs + 8 * side
        small_out[0][first : first + 8, :] = jnp.concatenate(found, axis=0)

    later_sum = (sub >= lane).astype(F32)
    sum_log = jnp.zeros((hp, 128), F32)
    sum_step = jnp.zeros((hp, 128), F32)
    for m in range(n):
        c = me ^ m
        rate_grad = dot(z1_ref[c], later_sum, NN, HIGHEST)
        step_grad = z2_ref[c] - e_log * rate_grad
        logit_grad = step_grad * sg_ref[c]
        sum_log = sum_log - step_ref[c] * e_log * rate_grad
        sum_step = sum_step + logit_grad
        small_out[m][:hp, :] = logit_grad
        big_out[m][...] = od_ref[rows_of(c), :]
        bc_out[m][...] = og_ref[rows_of(c), :]
    first = hp + 8 * pairs + 16
    small_out[0][first : first + hp, :] = sum_log
    small_out[0][first + hp : first + 2 * hp, :] = sum_step
    for m in range(1, n):
        small_out[m][hp:, :] = small_out[0][hp:, :]


def mixer_call(n, heads, hp, idx, doc, big, raw, steps, weight_x, bias_x, weight_bc, bias_bc, head_params):
    width = heads * MP
    pairs = width // 128
    wide = 2 - pairs % 2
    tokens = n * RB
    small_rows = 3 * hp + 8 * pairs + 16
    square = pltpu.VMEM((n, RB, RB), F32)
    square_low = pltpu.VMEM((n, RB, RB), BF16)
    flat = pltpu.VMEM((wide, tokens, 128), F32)
    flat_low = pltpu.VMEM((tokens, 128), BF16)
    per_head = pltpu.VMEM((n, hp, 128), F32)
    return pl.pallas_call(
        lambda *refs: mixer_kernel(n, heads, hp, *refs),
        out_shape=[jax.ShapeDtypeStruct((RB, 2 * width), BF16)] * n
        + [jax.ShapeDtypeStruct((RB, 256), BF16)] * n
        + [jax.ShapeDtypeStruct((small_rows, 128), F32)] * n,
        in_specs=[smem(), smem()] + [vmem()] * (3 * n + 5),
        out_specs=[vmem()] * (3 * n),
        scratch_shapes=[
            pltpu.VMEM((tokens, 2 * width), BF16),
            pltpu.VMEM((tokens, 2 * width), BF16),
            pltpu.VMEM((tokens + 8, 256), F32),
            pltpu.VMEM((tokens, 256), BF16),
            pltpu.VMEM((tokens + 8, 128), jnp.int32),
            pltpu.VMEM((wide, tokens + 8, 128), F32),
            pltpu.VMEM((wide, KC - 1, tokens + 8, 128), F32),
            flat_low,
            flat_low,
            square_low,
            square_low,
            square,
            square,
            square,
            square,
            square,
            per_head,
            per_head,
            per_head,
            per_head,
            per_head,
            pltpu.VMEM((wide, n + 1, 128, 128), F32),
            flat,
            flat,
            flat,
            flat,
            flat,
            flat,
            pltpu.VMEM((wide, tokens, 128), BF16),
            pltpu.VMEM((wide, n, 8, 128), F32),
            pltpu.VMEM((wide, KC + 2, 8, 128), F32),
        ],
        compiler_params=params(),
        name="mixer",
    )(idx, doc, *big, *raw, *steps, weight_x, bias_x, weight_bc, bias_bc, head_params)


def program(
    mixer_x,
    mixer_bc,
    dt_raw,
    gate_z,
    conv_weight_x,
    conv_bias_x,
    conv_weight_bc,
    conv_bias_bc,
    a_log,
    dt_bias,
    skip_d,
    d_mixer,
    doc_lengths,
    att_queries,
    att_keys,
    att_values,
    d_attn,
):
    n = lax.axis_size("ctx")
    place = lax.axis_index("ctx")
    idx = jnp.reshape(place, (1,)).astype(jnp.int32)
    rows, channels = mixer_x.shape
    all_heads = channels // MP
    heads = all_heads // n
    hp = max(8, heads)
    reach = max(1, n // 2)

    packed = pack_call(n, idx, mixer_x, gate_z, d_mixer)
    big = [packed[0]] + [crossed(packed[m], "ctx", m) for m in range(1, n)]

    own = jnp.concatenate([att_keys, att_values], axis=1)
    logits = jnp.transpose(dt_raw).reshape(n, heads, rows)
    logits = jnp.pad(logits, ((0, 0), (0, hp - heads), (0, 0)))
    own, raw_own, logits, _ = lax.optimization_barrier((own, mixer_bc, logits, packed[0]))
    blocks = [shifted(own, "ctx", d) for d in range(reach, 0, -1)] + [own]
    raw = [raw_own] + [crossed(raw_own, "ctx", m) for m in range(1, n)]
    steps = [lax.dynamic_index_in_dim(logits, place ^ m, 0, keepdims=False) for m in range(n)]
    steps = [steps[0]] + [crossed(steps[m], "ctx", m) for m in range(1, n)]

    attended = attention_call(idx, doc_lengths, att_queries, d_attn, blocks)
    grad_queries = attended[0]
    grad_kv = attended[-1]
    for d in range(1, reach + 1):
        grad_kv = grad_kv + shifted(attended[1 + reach - d], "ctx", -d).astype(F32)
    kv_width = att_keys.shape[1]
    grad_keys = grad_kv[:, :kv_width].astype(BF16)
    grad_values = grad_kv[:, kv_width:].astype(BF16)

    head_params = jnp.stack([a_log, dt_bias, skip_d])
    head_params = lax.dynamic_slice_in_dim(head_params, place * heads, heads, 1)
    head_params = jnp.pad(head_params, ((0, 0), (0, hp - heads)))
    head_params = jnp.broadcast_to(head_params[:, :, None], (3, hp, 128))
    results = mixer_call(
        n,
        heads,
        hp,
        idx,
        doc_lengths,
        big,
        raw,
        steps,
        conv_weight_x,
        conv_bias_x[None],
        conv_weight_bc,
        conv_bias_bc[None],
        head_params,
    )
    bc_parts = [results[n]] + [crossed(results[n + m], "ctx", m) for m in range(1, n)]
    small = [results[2 * n]] + [crossed(results[2 * n + m], "ctx", m) for m in range(1, n)]
    big = [results[0]] + [crossed(results[m], "ctx", m) for m in range(1, n)]

    pairs = heads * MP // 128
    first = hp + 8 * pairs
    bc_sum = bc_parts[0].astype(F32)
    tap_sum = small[0][first : first + 16]
    for m in range(1, n):
        bc_sum = bc_sum + bc_parts[m].astype(F32)
        tap_sum = tap_sum + small[m][first : first + 16]
    tap_sum = jnp.concatenate([tap_sum[:8], tap_sum[8:]], axis=1)
    both = jnp.concatenate([bc_sum, tap_sum], axis=0)
    for m in range(1, lax.axis_size("head")):
        arrived = crossed(both, "head", m)
        total = arrived if m == 1 else total + arrived
    both = both + total
    grad_bc = both[:rows].astype(BF16)
    grad_weight_bc = both[rows : rows + KC]
    grad_bias_bc = both[rows + KC]

    grad_x, grad_z, taps, logit_rows, head_sums = unpack_call(n, hp, idx, gate_z, d_mixer, big, small)
    logit_rows = logit_rows.reshape(n, hp, rows)[:, :heads].reshape(all_heads, rows)
    head_sums = head_sums.reshape(n, hp, 2, 128)[:, :heads].sum(axis=-1).reshape(all_heads, 2)
    return (
        grad_x,
        grad_bc,
        jnp.transpose(logit_rows),
        grad_z,
        taps[:KC],
        taps[KC],
        grad_weight_bc,
        grad_bias_bc,
        head_sums[:, 0],
        head_sums[:, 1],
        taps[KC + 1].reshape(all_heads, MP).sum(axis=1),
        grad_queries,
        grad_keys,
        grad_values,
    )


def solution(mesh):
    placed = (
        P("ctx", "head"),
        P("ctx", None),
        P("ctx", "head"),
        P("ctx", "head"),
        P(None, "head"),
        P("head"),
        P(),
        P(),
        P("head"),
        P("head"),
        P("head"),
        P("ctx", "head"),
        P(),
        P("ctx", "head"),
        P("ctx", "head"),
        P("ctx", "head"),
        P("ctx", "head"),
    )
    return jax.shard_map(
        program,
        mesh=mesh,
        in_specs=placed,
        out_specs=(
            P("ctx", "head"),
            P("ctx", None),
            P("ctx", "head"),
            P("ctx", "head"),
            P(None, "head"),
            P("head"),
            P(),
            P(),
            P("head"),
            P("head"),
            P("head"),
            P("ctx", "head"),
            P("ctx", "head"),
            P("ctx", "head"),
        ),
        check_vma=False,
    )
```

```python
import math

import jax
import jax.numpy as jnp
from jax import lax
from jax.experimental import pallas as pl
from jax.experimental.pallas import tpu as pltpu
from jax.sharding import PartitionSpec as P


MP = 64
KC = 4
AH = 64
KVH = 8
HD = 128
RB = 128
FILL = -1e30
F32 = jnp.float32
BF16 = jnp.bfloat16
HIGHEST = lax.Precision.HIGHEST


def params(limit=56):
    return pltpu.CompilerParams(vmem_limit_bytes=limit * 1024 * 1024)


def shifted(value, axis, steps):
    count = lax.axis_size(axis)
    initial, last = (max(0, -steps), min(count, count - steps))
    return lax.ppermute(value, axis, [(source, source + steps) for source in range(initial, last)])


def crossed(value, axis, mask):
    count = lax.axis_size(axis)
    return lax.ppermute(value, axis, [(source, source ^ mask) for source in range(count)])


def dot(a, b, dims=((1,), (0,)), precision=None):
    return lax.dot_general(a, b, (dims, ((), ())), precision=precision, preferred_element_type=F32)


NN = ((1,), (0,))
NT = ((1,), (1,))
TN = ((0,), (0,))


def iota(shape, dim):
    return lax.broadcasted_iota(jnp.int32, shape, dim)


def doc_start(doc_ref, pos):
    end = jnp.int32(0)
    start = jnp.zeros_like(pos)
    for j in range(doc_ref.shape[0]):
        end = end + doc_ref[j]
        start = jnp.where(pos >= end, end, start)
    return start


def smem():
    return pl.BlockSpec(memory_space=pltpu.SMEM)


def vmem():
    return pl.BlockSpec(memory_space=pltpu.VMEM)


def attention_kernel(reach, idx_ref, doc_ref, q_ref, do_ref, *rest):
    nb = reach + 1
    kv_refs = rest[:nb]
    dq_ref = rest[nb]
    out_refs = rest[nb + 1 : 2 * nb + 1]
    k_ref, v_ref, kt_ref, mask_ref, qc_ref, dc_ref, p_ref, g_ref = rest[2 * nb + 1 :]
    group = AH // KVH
    kv_count = q_ref.shape[1] // (group * HD)
    inv_root = 1.0 / math.sqrt(HD)
    keys = nb * RB
    first = idx_ref[1] * RB
    q_pos = first + iota((8, RB), 1)
    q_start = doc_start(doc_ref, q_pos)[:1]
    k_pos = first - reach * RB + iota((keys, RB), 0)
    allowed = (k_pos <= q_pos[:1]) & (k_pos >= q_start)
    mask_ref[...] = jnp.where(allowed, 0.0, FILL)
    for kv in range(kv_count):
        for b in range(nb):
            k_ref[pl.ds(b * RB, RB), :] = kv_refs[b][:RB, pl.ds(kv * HD, HD)]
            v_ref[pl.ds(b * RB, RB), :] = kv_refs[b][:RB, pl.ds((kv_count + kv) * HD, HD)]
        kt_ref[...] = k_ref[...].astype(F32).T.astype(BF16)

        def one(h):
            lanes = pl.ds(pl.multiple_of((kv * group + h) * HD, HD), HD)
            rows = pl.ds(pl.multiple_of(h * RB, RB), RB)
            q = q_ref[:, lanes]
            do = do_ref[:, lanes]
            qc_ref[rows, :] = q
            dc_ref[rows, :] = do
            scores = dot(k_ref[...], q, NT) * inv_root + mask_ref[...]
            top = jnp.max(scores, axis=0, keepdims=True)
            weights = jnp.exp(scores - top)
            softmax = weights * (1.0 / jnp.sum(weights, axis=0, keepdims=True))
            grad_prob = dot(v_ref[...], do, NT)
            delta = jnp.sum(softmax * grad_prob, axis=0, keepdims=True)
            grad_score = (softmax * (grad_prob - delta)).astype(BF16)
            p_ref[:, rows] = softmax.astype(BF16)
            g_ref[:, rows] = grad_score
            grad_q = dot(kt_ref[...], grad_score, NN) * inv_root
            dq_ref[:, lanes] = grad_q.T.astype(BF16)

        def head(h, carry):
            one(2 * h)
            one(2 * h + 1)
            return carry

        lax.fori_loop(0, group // 2, head, 0)
        grad_k = dot(g_ref[...], qc_ref[...], NN) * inv_root
        grad_v = dot(p_ref[...], dc_ref[...], NN)
        for b in range(nb):
            kind = out_refs[b].dtype
            rows = slice(b * RB, (b + 1) * RB)
            out_refs[b][:, pl.ds(kv * HD, HD)] = grad_k[rows].astype(kind)
            out_refs[b][:, pl.ds((kv_count + kv) * HD, HD)] = grad_v[rows].astype(kind)


def attention_call(idx, doc, queries, grads, blocks):
    nb = len(blocks)
    keys = nb * RB
    group = AH // KVH
    outs = [jax.ShapeDtypeStruct(queries.shape, BF16)]
    outs += [jax.ShapeDtypeStruct(blocks[-1].shape, BF16)] * (nb - 1)
    outs += [jax.ShapeDtypeStruct(blocks[-1].shape, F32)]
    return pl.pallas_call(
        lambda *refs: attention_kernel(nb - 1, *refs),
        out_shape=outs,
        in_specs=[smem(), smem()] + [vmem()] * (2 + nb),
        out_specs=[vmem()] * (1 + nb),
        scratch_shapes=[
            pltpu.VMEM((keys, HD), BF16),
            pltpu.VMEM((keys, HD), BF16),
            pltpu.VMEM((HD, keys), BF16),
            pltpu.VMEM((keys, RB), F32),
            pltpu.VMEM((group * RB, HD), BF16),
            pltpu.VMEM((group * RB, HD), BF16),
            pltpu.VMEM((keys, group * RB), BF16),
            pltpu.VMEM((keys, group * RB), BF16),
        ],
        compiler_params=params(),
        name="attention",
    )(idx, doc, queries, grads, *blocks)


def pack_kernel(n, heads, idx_ref, x_ref, z_ref, d_ref, raw_ref, step_ref, *outs):
    width = heads * MP
    me = idx_ref[0]
    lane = iota((x_ref.shape[0], 128), 1)
    for m in range(n):
        dest = me ^ m
        lanes = pl.ds(pl.multiple_of(dest * width, 128), width)
        z = z_ref[:, lanes].astype(F32)
        grad = d_ref[:, lanes].astype(F32) * z * jax.nn.sigmoid(z)
        outs[m][:, :width] = x_ref[:, lanes]
        outs[m][:, width : 2 * width] = grad.astype(BF16)
        outs[m][:, 2 * width : 2 * width + 256] = raw_ref[...]
        logit = pltpu.roll(step_ref[...], (128 - dest * heads) % 128, 1)
        high = logit.astype(BF16).astype(F32)
        middle = (logit - high).astype(BF16).astype(F32)
        rest = logit - high - middle
        parts = jnp.where(lane < heads, high, pltpu.roll(middle, heads, 1))
        parts = jnp.where(lane < 2 * heads, parts, pltpu.roll(rest, 2 * heads, 1))
        outs[m][:, 2 * width + 256 :] = parts.astype(BF16)


def pack_call(n, heads, idx, mixer_x, gate_z, d_mixer, raw, steps):
    rows = mixer_x.shape[0]
    return pl.pallas_call(
        lambda *refs: pack_kernel(n, heads, *refs),
        out_shape=[jax.ShapeDtypeStruct((rows, 2 * heads * MP + 384), BF16)] * n,
        in_specs=[smem()] + [vmem()] * 5,
        out_specs=[vmem()] * n,
        compiler_params=params(),
        name="pack",
    )(idx, mixer_x, gate_z, d_mixer, raw, steps)


def keys_kernel(n, k_ref, v_ref, x_ref, raw_ref, own_ref, *outs):
    kv_width = k_ref.shape[1]
    width = x_ref.shape[1] // n
    half = width // 2
    own_ref[:, :kv_width] = k_ref[...]
    own_ref[:, kv_width:] = v_ref[...]
    for d in range(n):
        outs[d][:RB, :kv_width] = k_ref[...]
        outs[d][:RB, kv_width:] = v_ref[...]
        outs[d][RB : RB + 16, :] = x_ref[:, d * width : d * width + half]
        outs[d][RB + 16 : RB + 32, :] = x_ref[:, d * width + half : (d + 1) * width]
        outs[d][RB + 32 :, :256] = raw_ref[...]
        if 2 * kv_width > 256:
            outs[d][RB + 32 :, 256:] = jnp.zeros((16, 2 * kv_width - 256), BF16)


def keys_call(n, att_keys, att_values, mixer_x, mixer_bc):
    rows, kv_width = att_keys.shape
    last = rows // 16 - 1
    return pl.pallas_call(
        lambda *refs: keys_kernel(n, *refs),
        grid=(1,),
        out_shape=[jax.ShapeDtypeStruct((rows, 2 * kv_width), BF16)]
        + [jax.ShapeDtypeStruct((rows + 48, 2 * kv_width), BF16)] * n,
        in_specs=[
            pl.BlockSpec((rows, kv_width), lambda i: (0, 0)),
            pl.BlockSpec((rows, kv_width), lambda i: (0, 0)),
            pl.BlockSpec((16, mixer_x.shape[1]), lambda i: (last, 0)),
            pl.BlockSpec((16, 256), lambda i: (last, 0)),
        ],
        out_specs=[pl.BlockSpec((rows, 2 * kv_width), lambda i: (0, 0))]
        + [pl.BlockSpec((rows + 48, 2 * kv_width), lambda i: (0, 0))] * n,
        compiler_params=params(),
        name="keys",
    )(att_keys, att_values, mixer_x, mixer_bc)


def edges_kernel(n, hp, pairs, idx_ref, *refs):
    edges = refs[:n]
    logit_ref, margin_ref, share_ref, rows_ref = refs[n:]
    width = pairs * 128
    me = idx_ref[0]
    margin = jnp.zeros((16, 128), F32)
    total = jnp.zeros((16, 128), F32)
    first = hp + 8 * pairs + 16
    heads_at = first + 8 * pairs + 16
    for m in range(n):
        source = me ^ m
        held = pl.ds(pl.multiple_of(source * hp, 8), hp)
        rows_ref[0, held, :] = edges[m][:hp, :]
        for k in range(3):
            rows_ref[1 + k, held, :] = edges[m][heads_at + k * hp : heads_at + (k + 1) * hp, :]
        for p in range(pairs):
            part = pl.ds(pl.multiple_of(source * width + p * 128, 128), 128)
            margin_ref[:, part] = edges[m][hp + 8 * p : hp + 8 * p + 8, :]
            share_ref[:, part] = edges[m][first + 8 * p : first + 8 * p + 8, :]
        margin = margin + edges[m][hp + 8 * pairs : first, :]
        total = total + edges[m][first + 8 * pairs : heads_at, :]
    at = n * width
    margin_ref[:, at : at + 128] = margin[:8]
    margin_ref[:, at + 128 :] = margin[8:]
    share_ref[:, at : at + 128] = total[:8]
    share_ref[:, at + 128 : at + 256] = total[8:]
    ones = jnp.ones((8, 128), F32)
    for k in range(3):
        lanes = slice(at + 256 + k * n * hp, at + 256 + (k + 1) * n * hp)
        share_ref[:, lanes] = dot(ones, rows_ref[1 + k], NT, HIGHEST)
    logit_ref[...] = rows_ref[0].T


def edges_call(n, hp, pairs, idx, edges):
    return pl.pallas_call(
        lambda *refs: edges_kernel(n, hp, pairs, *refs),
        out_shape=[
            jax.ShapeDtypeStruct((RB, n * hp), F32),
            jax.ShapeDtypeStruct((8, n * pairs * 128 + 256), F32),
            jax.ShapeDtypeStruct((8, n * pairs * 128 + 256 + 3 * n * hp), F32),
        ],
        in_specs=[smem()] + [vmem()] * n,
        out_specs=[vmem()] * 3,
        scratch_shapes=[pltpu.VMEM((4, n * hp, 128), F32)],
        compiler_params=params(),
        name="edges",
    )(idx, *edges)


def unpack_kernel(n, hp, idx_ref, z_ref, d_ref, margin_ref, share_ref, *refs):
    big = refs[:n]
    gx_ref, gz_ref, taps_ref, bias_ref, heads_ref = refs[n:]
    channels = z_ref.shape[1]
    width = channels // n
    me = idx_ref[0]
    use = jnp.where(me == n - 1, 1.0, 0.0)
    for m in range(n):
        source = me ^ m
        lanes = pl.ds(pl.multiple_of(source * width, 128), width)
        gx_ref[: RB - 16, lanes] = big[m][: RB - 16, :width]
        end = big[m][RB - 16 :, :width].astype(F32)
        end = jnp.concatenate([end[:8], end[8:] + use * margin_ref[:, lanes]], axis=0)
        gx_ref[RB - 16 :, lanes] = end.astype(BF16)
        z = z_ref[:, lanes].astype(F32)
        sig = jax.nn.sigmoid(z)
        y = big[m][:, width:].astype(F32)
        gz_ref[:, lanes] = (d_ref[:, lanes].astype(F32) * y * (sig * (1.0 + z * (1.0 - sig)))).astype(BF16)
    taps_ref[...] = share_ref[:KC, :channels]
    bias_ref[...] = share_ref[KC : KC + 1, :channels]
    for k in range(3):
        at = channels + 256 + k * n * hp
        heads_ref[k : k + 1, :] = share_ref[:1, at : at + n * hp]


def unpack_call(n, hp, idx, gate_z, d_mixer, margin, share, big):
    rows, channels = gate_z.shape
    return pl.pallas_call(
        lambda *refs: unpack_kernel(n, hp, *refs),
        out_shape=[
            jax.ShapeDtypeStruct((rows, channels), BF16),
            jax.ShapeDtypeStruct((rows, channels), BF16),
            jax.ShapeDtypeStruct((KC, channels), F32),
            jax.ShapeDtypeStruct((1, channels), F32),
            jax.ShapeDtypeStruct((3, n * hp), F32),
        ],
        in_specs=[smem()] + [vmem()] * (4 + n),
        out_specs=[vmem()] * 5,
        compiler_params=params(),
        name="unpack",
    )(idx, gate_z, d_mixer, margin, share, *big)


def by_sublane(value):
    return jnp.sum(value.reshape(value.shape[0] // 8, 8, value.shape[1]), axis=0)


class Shared:
    def __init__(self, n, heads, hp, idx_ref, doc_ref, ins, scratch, full):
        self.n = n
        self.me = me = idx_ref[0]
        first = (idx_ref[1] - me) * RB
        xd_in = ins[:n]
        tails = ins[n : 2 * n]
        self.wx_ref, self.bx_ref, wbc_ref, bbc_ref, par_ref = ins[2 * n :]
        self.par_ref = par_ref
        width = heads * MP
        self.tail_ref, self.xd_ref, self.raw_ref, self.off_ref, self.xs_ref = scratch[:5]
        self.bb_ref, self.cc_ref, self.bt_ref, self.ct_ref, self.step_ref, self.cum_ref = scratch[5:11]
        if full:
            self.cb_ref, self.bias_ref, self.sg_ref = scratch[11:14]
        self.lane = lane = iota((RB, 128), 1)
        self.sub = sub = iota((RB, 128), 0)
        self.low = lane < MP
        upper = (sub <= lane).astype(F32)
        self.e_log = e_log = jnp.exp(par_ref[0])
        for m in range(n):
            source = me ^ m
            self.tail_ref[m, :, : width // 2] = tails[m][RB : RB + 16, :]
            self.tail_ref[m, :, width // 2 : width] = tails[m][RB + 16 : RB + 32, :]
            self.tail_ref[m, :, width:] = tails[m][RB + 32 : RB + 48, :256]
            self.xd_ref[self.rows(source), :] = xd_in[m][:, : 2 * width]
            raw = xd_in[m][:, 2 * width : 2 * width + 256]
            self.raw_ref[pl.ds(pl.multiple_of(source * RB + 8, 8), RB), :] = raw.astype(F32)
            parts = xd_in[m][:, 2 * width + 256 :].astype(F32).T
            logit = parts[:hp] + parts[hp : 2 * hp] + parts[2 * hp : 3 * hp]
            logit = logit + par_ref[1]
            step = jnp.maximum(logit, 0.0) + jnp.log1p(jnp.exp(-jnp.abs(logit)))
            self.step_ref[source] = step
            if full:
                self.sg_ref[source] = jax.nn.sigmoid(logit)
            self.cum_ref[source] = dot(-step * e_log, upper, NN, HIGHEST)
        self.raw_ref[:8, :] = self.tail_ref[me, :, width:].astype(F32)[8:]
        self.wbc = wbc = wbc_ref[...]
        self.bbc = bbc = bbc_ref[...]

        def prepare(c, carry):
            pos = first + c * RB + sub
            off = pos - doc_start(doc_ref, pos)
            self.off_ref[self.rows(c), :] = off
            pre_b = self.conv(c, self.raw_ref, slice(0, 128), wbc[:, :128], bbc[:, :128])
            pre_c = self.conv(c, self.raw_ref, slice(128, 256), wbc[:, 128:], bbc[:, 128:])
            b_in = pre_b * jax.nn.sigmoid(pre_b)
            c_out = pre_c * jax.nn.sigmoid(pre_c)
            self.bt_ref[c] = b_in.T.astype(BF16)
            self.ct_ref[c] = c_out.T.astype(BF16)
            if full:
                allowed = (lane <= sub) & (sub - lane <= off)
                self.bias_ref[c] = jnp.where(allowed, 0.0, FILL)
                b_low, c_low = b_in.astype(BF16), c_out.astype(BF16)
                self.bb_ref[self.rows(c), :] = b_low
                self.cc_ref[self.rows(c), :] = c_low
                self.cb_ref[c] = dot(c_low, b_low, NT)
            return carry

        lax.fori_loop(0, n, prepare, 0)

    def rows(self, c, extra=0):
        return pl.ds(pl.multiple_of(c * RB, RB), RB + extra)

    def conv(self, c, src_ref, lanes, weight, bias):
        off = self.off_ref[self.rows(c), :]
        window = src_ref[self.rows(c, 8), lanes]
        pre = bias + weight[0:1] * window[8:]
        for j in range(1, KC):
            pre = pre + weight[j : j + 1] * jnp.where(off >= j, window[8 - j : 8 + RB - j], 0.0)
        return pre

    def load(self, u, lanes):
        self.xs_ref[u, :8, :] = self.tail_ref[self.me, :, lanes].astype(F32)[8:]

        def one(c, unused):
            rows = pl.ds(pl.multiple_of(c * RB + 8, 8), RB)
            self.xs_ref[u, rows, :] = self.xd_ref[self.rows(c), lanes].astype(F32)
            return unused

        lax.fori_loop(0, self.n, one, 0)

    def decays(self, last_off, off, cum):
        last = cum[RB - 1 :]
        enter = jnp.where(off > self.sub, jnp.exp(cum), 0.0)
        leave = jnp.where(self.sub >= RB - 1 - last_off, jnp.exp(last - cum), 0.0)
        keep = jnp.where(last_off >= RB, jnp.exp(last), 0.0)
        return enter, leave, keep

    def pair_rows(self, ref, c, p):
        return ref[c, pl.ds(2 * p, 1), :], ref[c, pl.ds(2 * p + 1, 1), :]


def shared_scratch(n, heads, hp, wide, full):
    width = heads * MP
    tokens = n * RB
    found = [
        pltpu.VMEM((n, 16, width + 256), BF16),
        pltpu.VMEM((tokens, 2 * width), BF16),
        pltpu.VMEM((tokens + 8, 256), F32),
        pltpu.VMEM((tokens, 128), jnp.int32),
        pltpu.VMEM((wide, tokens + 8, 128), F32),
        pltpu.VMEM((tokens, 128), BF16),
        pltpu.VMEM((tokens, 128), BF16),
        pltpu.VMEM((n, 128, RB), BF16),
        pltpu.VMEM((n, 128, RB), BF16),
        pltpu.VMEM((n, hp, 128), F32),
        pltpu.VMEM((n, hp, 128), F32),
    ]
    if full:
        found += [
            pltpu.VMEM((n, RB, RB), F32),
            pltpu.VMEM((n, RB, RB), F32),
            pltpu.VMEM((n, hp, 128), F32),
        ]
    return found


def totals_kernel(n, heads, hp, wide, idx_ref, doc_ref, *refs):
    pairs = heads * MP // 128
    width = heads * MP
    ins = refs[: 2 * n + 5]
    state_ref, grad_ref, keep_ref = refs[2 * n + 5 : 2 * n + 8]
    sh = Shared(n, heads, hp, idx_ref, doc_ref, ins, refs[2 * n + 8 :], False)

    def streams(block, carry):
        ids = [block * wide + u for u in range(wide)]
        held = [pl.ds(pl.multiple_of(sh.me * width + p * 128, 128), 128) for p in ids]
        weight = [sh.wx_ref[:, h] for h in held]
        bias = [sh.bx_ref[:, h] for h in held]
        for u in range(wide):
            sh.load(u, pl.ds(pl.multiple_of(ids[u] * 128, 128), 128))

        def one(u, c, state, grads, kept):
            p = ids[u]
            off = sh.off_ref[sh.rows(c), :]
            pre = sh.conv(c, sh.xs_ref.at[u], slice(None), weight[u], bias[u])
            x = pre * jax.nn.sigmoid(pre)
            row0, row1 = sh.pair_rows(sh.cum_ref, c, p)
            step0, step1 = sh.pair_rows(sh.step_ref, c, p)
            cum = jnp.where(sh.sub < MP, row0, row1).T
            step = jnp.where(sh.sub < MP, step0, step1).T
            enter, leave, keep = sh.decays(off[RB - 1 :], off, cum)
            grad = sh.xd_ref[sh.rows(c), pl.ds(pl.multiple_of(width + p * 128, 128), 128)].astype(F32)
            state = keep * state + dot(sh.bt_ref[c], (leave * (step * x)).astype(BF16), NN)
            grads = grads + kept * dot(sh.ct_ref[c], (enter * grad).astype(BF16), NN)
            return state, grads, kept * keep

        def chunk(c, held):
            return tuple(one(u, c, *held[u]) for u in range(wide))

        zero = jnp.zeros((128, 128), F32)
        found = lax.fori_loop(0, n, chunk, tuple((zero, zero, jnp.ones((1, 128), F32)) for _ in range(wide)))
        for u in range(wide):
            state_ref[ids[u]] = found[u][0].astype(BF16)
            grad_ref[ids[u]] = found[u][1].astype(BF16)
            keep_ref[ids[u]] = jnp.broadcast_to(found[u][2], (8, 128))
        return carry

    lax.fori_loop(0, pairs // wide, streams, 0)


def totals_call(n, heads, hp, idx, doc, ins):
    pairs = heads * MP // 128
    wide = 2 - pairs % 2
    return pl.pallas_call(
        lambda *refs: totals_kernel(n, heads, hp, wide, *refs),
        out_shape=[
            jax.ShapeDtypeStruct((pairs, 128, 128), BF16),
            jax.ShapeDtypeStruct((pairs, 128, 128), BF16),
            jax.ShapeDtypeStruct((pairs, 8, 128), F32),
        ],
        in_specs=[smem(), smem()] + [vmem()] * len(ins),
        out_specs=[vmem()] * 3,
        scratch_shapes=shared_scratch(n, heads, hp, wide, False),
        compiler_params=params(),
        name="totals",
    )(idx, doc, *ins)


def mixer_kernel(n, heads, hp, wide, idx_ref, doc_ref, *refs):
    width = heads * MP
    pairs = width // 128
    ins = refs[: 2 * n + 5]
    first_ref, later_ref = refs[2 * n + 5 : 2 * n + 7]
    at = 2 * n + 7
    big_out = refs[at : at + n]
    bc_out = refs[at + n : at + 2 * n]
    edge_out = refs[at + 2 * n : at + 3 * n]
    at = at + 3 * n
    (
        od_ref,
        og_ref,
        gp_ref,
        dcb_ref,
        db_ref,
        dc_ref,
        z1_ref,
        z2_ref,
        sin_ref,
        yn_ref,
        dwi_ref,
        lv_ref,
        st_ref,
        xc_ref,
        ds_ref,
        ed_ref,
        k_ref,
        acc_ref,
        skip_ref,
    ) = refs[at : at + 19]
    sh = Shared(n, heads, hp, idx_ref, doc_ref, ins, refs[at + 19 :], True)
    me, lane, sub, low = sh.me, sh.lane, sh.sub, sh.low
    par_ref, wx_ref, bx_ref, xd_ref, off_ref = sh.par_ref, sh.wx_ref, sh.bx_ref, sh.xd_ref, sh.off_ref
    raw_ref, xs_ref, cum_ref, step_ref = sh.raw_ref, sh.xs_ref, sh.cum_ref, sh.step_ref
    bb_ref, cc_ref, bt_ref, ct_ref = sh.bb_ref, sh.cc_ref, sh.bt_ref, sh.ct_ref
    cb_ref, bias_ref, sg_ref = sh.cb_ref, sh.bias_ref, sh.sg_ref
    wbc, bbc, e_log, conv, rows_of = sh.wbc, sh.bbc, sh.e_log, sh.conv, sh.rows
    tokens = n * RB
    sums_at = hp + 8 * pairs + 16
    zero8 = jnp.zeros((8, 128), F32)
    for c in range(n):
        z1_ref[c] = jnp.zeros((hp, 128), F32)
        z2_ref[c] = jnp.zeros((hp, 128), F32)
        dcb_ref[c] = jnp.zeros((RB, RB), F32)
        db_ref[c] = jnp.zeros((RB, 128), F32)
        dc_ref[c] = jnp.zeros((RB, 128), F32)
    skip_ref[...] = jnp.zeros((hp, 128), F32)
    for u in range(wide):
        for j in range(KC - 1):
            gp_ref[u, j, tokens:, :] = zero8

    def conv_back(c, grad, src_ref, lanes, weight, u):
        off = off_ref[rows_of(c), :]
        window = src_ref[rows_of(c, 8), lanes]
        back = weight[0:1] * grad
        sums = [by_sublane(grad * window[8:])]
        for j in range(1, KC):
            held_back = jnp.where(off >= j, grad, 0.0)
            sums.append(by_sublane(held_back * window[8 - j : 8 + RB - j]))
            gp_ref[u, j - 1, rows_of(c), :] = held_back
            back = back + weight[j : j + 1] * gp_ref[u, j - 1, rows_of(c, 8), :][j : j + RB]
        sums.append(by_sublane(grad))
        return back, sums

    def silu_parts(pre):
        sig = jax.nn.sigmoid(pre)
        return pre * sig, sig * (1.0 + pre * (1.0 - sig))

    def margin_of(weight, u):
        total = zero8
        for j in range(1, KC):
            turned = pltpu.roll(gp_ref[u, j - 1, :8, :], 8 - j, 0)
            total = total + weight[j : j + 1] * jnp.where(sub[:8] >= 8 - j, turned, 0.0)
        return total

    def streams(block, carry):
        ids = [block * wide + u for u in range(wide)]
        each = range(wide)
        lanes = [pl.ds(pl.multiple_of(p * 128, 128), 128) for p in ids]
        lanes_d = [pl.ds(pl.multiple_of(width + p * 128, 128), 128) for p in ids]
        held = [pl.ds(pl.multiple_of(me * width + p * 128, 128), 128) for p in ids]
        weight = [wx_ref[:, h] for h in held]
        bias = [bx_ref[:, h] for h in held]
        skip = [
            jnp.where(low[:1], par_ref[2, pl.ds(2 * p, 1), :], par_ref[2, pl.ds(2 * p + 1, 1), :]) for p in ids
        ]
        pick = [
            jnp.where(iota((hp, 128), 0) == 2 * p + iota((hp, 128), 1) // MP, 1.0, 0.0).astype(BF16) for p in ids
        ]

        for u in each:
            sh.load(u, lanes[u])

        def forward_one(u, c, state):
            p = ids[u]
            rows = rows_of(c)
            off = off_ref[rows, :]
            pre = conv(c, xs_ref.at[u], slice(None), weight[u], bias[u])
            x, slope = silu_parts(pre)
            xc_ref[u, rows, :] = x
            ds_ref[u, rows, :] = slope
            row0 = cum_ref[c, pl.ds(2 * p, 1), :]
            row1 = cum_ref[c, pl.ds(2 * p + 1, 1), :]
            col0 = jnp.broadcast_to(row0, (128, RB)).T
            col1 = jnp.broadcast_to(row1, (128, RB)).T
            step0 = step_ref[c, pl.ds(2 * p, 1), :]
            step1 = step_ref[c, pl.ds(2 * p + 1, 1), :]
            step = jnp.where(sub < MP, step0, step1).T
            st_ref[u, rows, :] = step
            cum = jnp.where(low, col0, col1)
            mask = bias_ref[c]
            cb = cb_ref[c]
            decay0 = jnp.exp(col0 - row0 + mask)
            decay1 = jnp.exp(col1 - row1 + mask)
            mix0 = (decay0 * cb).astype(BF16)
            mix1 = (decay1 * cb).astype(BF16)
            value = step * x
            grad = xd_ref[rows, lanes_d[u]].astype(F32)
            value_low = value.astype(BF16)
            value_two = jnp.concatenate(
                [jnp.where(low, value, 0.0).astype(BF16), jnp.where(low, 0.0, value).astype(BF16)], axis=0
            )
            grad_two = jnp.concatenate(
                [jnp.where(low, grad, 0.0).astype(BF16), jnp.where(low, 0.0, grad).astype(BF16)], axis=0
            )
            inner = dot(jnp.concatenate([mix0, mix1], axis=1), value_two, NN)
            dwi_ref[u, rows, :] = dot(jnp.concatenate([mix0, mix1], axis=0), grad_two, TN)
            grad_mix = dot(grad_two, value_low, NT)
            added = decay0 * grad_mix[:RB] + decay1 * grad_mix[RB:]
            enter, leave, keep = sh.decays(off[RB - 1 :], off, cum)
            lv_ref[u, rows, :] = leave
            k_ref[u, c] = jnp.broadcast_to(keep, (8, 128))
            sin_ref[u, c] = state
            state_low = state.astype(BF16)
            total = inner + enter * dot(cc_ref[rows, :], state_low, NN)
            yn_ref[u, rows, :] = total
            od_ref[rows, lanes_d[u]] = (total + skip[u] * x).astype(BF16)
            entered = (enter * grad).astype(BF16)
            ed_ref[u, rows, :] = entered
            new_state = keep * state + dot(bt_ref[c], (leave * value).astype(BF16), NN)
            return new_state, added, dot(entered, state_low, NT)

        def forward(c, states):
            found = [forward_one(u, c, states[u]) for u in each]
            dcb_ref[c] += sum(f[1] for f in found)
            dc_ref[c] += sum(f[2] for f in found)
            return tuple(f[0] for f in found)

        final = lax.fori_loop(0, n, forward, tuple(first_ref[p].astype(F32) for p in ids))
        for u in each:
            sin_ref[u, n] = final[u]
            for j in range(KC + 2):
                acc_ref[u, j] = zero8

        def backward_one(u, c, later):
            rows = rows_of(c)
            later_low = later.astype(BF16)
            leave = lv_ref[u, rows, :]
            x = xc_ref[u, rows, :]
            step = st_ref[u, rows, :]
            grad = xd_ref[rows, lanes_d[u]].astype(F32)
            value = step * x
            grad_value = dwi_ref[u, rows, :] + leave * dot(bb_ref[rows, :], later_low, NN)
            z1 = grad * yn_ref[u, rows, :] - value.astype(BF16).astype(F32) * grad_value
            carried = jnp.sum(later_low.astype(F32) * sin_ref[u, c + 1], axis=0, keepdims=True)
            z1 = jnp.concatenate([z1[: RB - 8], z1[RB - 8 :] + jnp.where(sub[RB - 8 :] == RB - 1, carried, 0.0)], axis=0)
            z1_high = z1.astype(BF16)
            z1_rest = (z1 - z1_high.astype(F32)).astype(BF16)
            rates = dot(pick[u], z1_high, NT) + dot(pick[u], z1_rest, NT)
            steps = dot(pick[u], (x * grad_value).astype(BF16), NT)
            grad_b = dot((leave * value).astype(BF16), later_low, NT)
            grad_x = (step * grad_value + skip[u] * grad) * ds_ref[u, rows, :]
            back, sums = conv_back(c, grad_x, xs_ref.at[u], slice(None), weight[u], u)
            od_ref[rows, lanes[u]] = back.astype(BF16)
            sums.append(by_sublane(grad * x))
            for j in range(KC + 2):
                acc_ref[u, j] += sums[j]
            new_later = k_ref[u, c][:1] * later + dot(ct_ref[c], ed_ref[u, rows, :], NN)
            return new_later, rates, steps, grad_b

        def backward(k, laters):
            c = n - 1 - k
            found = [backward_one(u, c, laters[u]) for u in each]
            z1_ref[c] += sum(f[1] for f in found)
            z2_ref[c] += sum(f[2] for f in found)
            db_ref[c] += sum(f[3] for f in found)
            return tuple(f[0] for f in found)

        lax.fori_loop(0, n, backward, tuple(later_ref[p].astype(F32) for p in ids))
        for u in each:
            found = [jnp.sum(acc_ref[u, j], axis=0, keepdims=True) for j in range(KC + 2)]
            skip_ref[...] += pick[u].astype(F32) * found[KC + 1]
            found = found[: KC + 1] + [jnp.zeros((8 - KC - 1, 128), F32)]
            edge_out[0][pl.ds(pl.multiple_of(sums_at + 8 * ids[u], 8), 8), :] = jnp.concatenate(found, axis=0)
            edge_out[0][pl.ds(pl.multiple_of(hp + 8 * ids[u], 8), 8), :] = margin_of(weight[u], u)
        return carry

    lax.fori_loop(0, pairs // wide, streams, 0)

    for side in range(2):
        lanes = slice(128 * side, 128 * side + 128)
        weight = wbc[:, lanes]
        bias = bbc[:, lanes]
        for j in range(KC + 1):
            acc_ref[0, j] = zero8

        def finish(k, carry):
            c = n - 1 - k
            rows = rows_of(c)
            mixed = dcb_ref[c].astype(BF16)
            if side == 0:
                grad = db_ref[c] + dot(mixed, cc_ref[rows, :], TN)
            else:
                grad = dc_ref[c] + dot(mixed, bb_ref[rows, :], NN)
            pre = conv(c, raw_ref, lanes, weight, bias)
            back, sums = conv_back(c, grad * silu_parts(pre)[1], raw_ref, lanes, weight, 0)
            og_ref[rows, lanes] = back.astype(BF16)
            for j in range(KC + 1):
                acc_ref[0, j] += sums[j]
            return carry

        lax.fori_loop(0, n, finish, 0)
        found = [jnp.sum(acc_ref[0, j], axis=0, keepdims=True) for j in range(KC + 1)]
        found.append(jnp.zeros((8 - KC - 1, 128), F32))
        at_row = 8 * pairs + 8 * side
        edge_out[0][sums_at + at_row : sums_at + at_row + 8, :] = jnp.concatenate(found, axis=0)
        edge_out[0][hp + at_row : hp + at_row + 8, :] = margin_of(weight, 0)

    later_sum = (sub >= lane).astype(F32)
    sum_log = jnp.zeros((hp, 128), F32)
    sum_step = jnp.zeros((hp, 128), F32)
    for m in range(n):
        c = me ^ m
        rate_grad = dot(z1_ref[c], later_sum, NN, HIGHEST)
        step_grad = z2_ref[c] - e_log * rate_grad
        logit_grad = step_grad * sg_ref[c]
        sum_log = sum_log - step_ref[c] * e_log * rate_grad
        sum_step = sum_step + logit_grad
        edge_out[m][:hp, :] = logit_grad
        big_out[m][...] = od_ref[rows_of(c), :]
        bc_out[m][...] = og_ref[rows_of(c), :]
    at_row = sums_at + 8 * pairs + 16
    edge_out[0][at_row : at_row + hp, :] = sum_log
    edge_out[0][at_row + hp : at_row + 2 * hp, :] = sum_step
    edge_out[0][at_row + 2 * hp : at_row + 3 * hp, :] = skip_ref[...]
    for m in range(1, n):
        edge_out[m][hp:, :] = edge_out[0][hp:, :]


def mixer_call(n, heads, hp, idx, doc, ins, first, later):
    width = heads * MP
    pairs = width // 128
    wide = 2 - pairs % 2
    tokens = n * RB
    square = pltpu.VMEM((n, RB, RB), F32)
    flat = pltpu.VMEM((wide, tokens, 128), F32)
    per_head = pltpu.VMEM((n, hp, 128), F32)
    return pl.pallas_call(
        lambda *refs: mixer_kernel(n, heads, hp, wide, *refs),
        out_shape=[jax.ShapeDtypeStruct((RB, 2 * width), BF16)] * n
        + [jax.ShapeDtypeStruct((RB, 256), BF16)] * n
        + [jax.ShapeDtypeStruct((4 * hp + 16 * pairs + 32, 128), F32)] * n,
        in_specs=[smem(), smem()] + [vmem()] * (len(ins) + 2),
        out_specs=[vmem()] * (3 * n),
        scratch_shapes=[
            pltpu.VMEM((tokens, 2 * width), BF16),
            pltpu.VMEM((tokens, 256), BF16),
            pltpu.VMEM((wide, KC - 1, tokens + 8, 128), F32),
            square,
            square,
            square,
            per_head,
            per_head,
            pltpu.VMEM((wide, n + 1, 128, 128), F32),
            flat,
            flat,
            flat,
            flat,
            flat,
            flat,
            pltpu.VMEM((wide, tokens, 128), BF16),
            pltpu.VMEM((wide, n, 8, 128), F32),
            pltpu.VMEM((wide, KC + 2, 8, 128), F32),
            pltpu.VMEM((hp, 128), F32),
        ]
        + shared_scratch(n, heads, hp, wide, True),
        compiler_params=params(),
        name="mixer",
    )(idx, doc, *ins, first, later)


def program(
    mixer_x,
    mixer_bc,
    dt_raw,
    gate_z,
    conv_weight_x,
    conv_bias_x,
    conv_weight_bc,
    conv_bias_bc,
    a_log,
    dt_bias,
    skip_d,
    d_mixer,
    doc_lengths,
    att_queries,
    att_keys,
    att_values,
    d_attn,
):
    n = lax.axis_size("ctx")
    group = min(4, n)
    place = lax.axis_index("ctx")
    inside = place % group
    idx = jnp.stack([inside, place]).astype(jnp.int32)
    rows, channels = mixer_x.shape
    all_heads = channels // MP
    heads = all_heads // group
    hp = heads
    width = heads * MP
    pairs = width // 128
    reach = max(1, n // 2)

    sent = keys_call(group, att_keys, att_values, mixer_x, mixer_bc)
    own = sent[0]
    reached = [shifted(sent[d] if d <= group else own, "ctx", d) for d in range(1, max(reach, group) + 1)]
    tails = reached[:group]
    blocks = reached[:reach][::-1] + [own]

    logits = jnp.pad(dt_raw, ((0, 0), (0, 128 - all_heads)))
    packed = pack_call(group, heads, idx, mixer_x, gate_z, d_mixer, mixer_bc, logits)
    big = [packed[0]] + [crossed(packed[m], "ctx", m) for m in range(1, group)]

    head_params = jnp.stack([a_log, dt_bias, skip_d])
    head_params = lax.dynamic_slice_in_dim(head_params, inside * heads, heads, 1)
    head_params = jnp.broadcast_to(head_params[:, :, None], (3, hp, 128))
    ins = (
        big
        + tails
        + [conv_weight_x, conv_bias_x[None], conv_weight_bc, conv_bias_bc[None], head_params]
    )
    state, grad_state, keep = totals_call(group, heads, hp, idx, doc_lengths, ins)
    back_state, back_keep = grad_state, keep
    covered = 1
    while covered < n // group // 2:
        step_by = covered * group
        state = (state.astype(F32) + keep[:, :1] * shifted(state, "ctx", step_by).astype(F32)).astype(BF16)
        back_state = (
            back_state.astype(F32) + back_keep[:, :1] * shifted(back_state, "ctx", -step_by).astype(F32)
        ).astype(BF16)
        keep = keep * shifted(keep, "ctx", step_by)
        back_keep = back_keep * shifted(back_keep, "ctx", -step_by)
        covered = 2 * covered
    first = shifted(state, "ctx", group)
    later = shifted(back_state, "ctx", -group)

    attended = attention_call(idx, doc_lengths, att_queries, d_attn, blocks)
    grad_queries = attended[0]
    grad_kv = attended[-1]
    arrived = [shifted(attended[1 + reach - d], "ctx", -d) for d in range(1, reach + 1)]
    for part in arrived:
        grad_kv = grad_kv + part.astype(F32)
    kv_width = att_keys.shape[1]
    grad_keys = grad_kv[:, :kv_width].astype(BF16)
    grad_values = grad_kv[:, kv_width:].astype(BF16)

    results = mixer_call(group, heads, hp, idx, doc_lengths, ins, first, later)
    edges = [results[2 * group]] + [crossed(results[2 * group + m], "ctx", m) for m in range(1, group)]
    bc_parts = [results[group]] + [crossed(results[group + m], "ctx", m) for m in range(1, group)]
    big = [results[0]] + [crossed(results[m], "ctx", m) for m in range(1, group)]

    grad_logits, margin, share = edges_call(group, hp, pairs, idx, edges)
    margin = shifted(margin, "ctx", -1)
    mask = group
    while mask < n:
        share = share + crossed(share, "ctx", mask)
        mask = 2 * mask

    bc_sum = bc_parts[0].astype(F32)
    for m in range(1, group):
        bc_sum = bc_sum + bc_parts[m].astype(F32)
    bc_margin = jnp.where(inside == group - 1, margin[:, channels:], 0.0)
    bc_sum = jnp.concatenate([bc_sum[: rows - 8], bc_sum[rows - 8 :] + bc_margin], axis=0)
    both = jnp.concatenate([bc_sum, share[:, channels : channels + 256]], axis=0)
    total = both
    for m in range(1, lax.axis_size("head")):
        total = total + crossed(both, "head", m)
    grad_bc = total[:rows].astype(BF16)
    grad_weight_bc = total[rows : rows + KC]
    grad_bias_bc = total[rows + KC]

    grad_x, grad_z, taps, bias_sum, head_sums = unpack_call(group, hp, idx, gate_z, d_mixer, margin, share, big)
    return (
        grad_x,
        grad_bc,
        grad_logits,
        grad_z,
        taps,
        bias_sum[0],
        grad_weight_bc,
        grad_bias_bc,
        head_sums[0],
        head_sums[1],
        head_sums[2],
        grad_queries,
        grad_keys,
        grad_values,
    )


def solution(mesh):
    placed = (
        P("ctx", "head"),
        P("ctx", None),
        P("ctx", "head"),
        P("ctx", "head"),
        P(None, "head"),
        P("head"),
        P(),
        P(),
        P("head"),
        P("head"),
        P("head"),
        P("ctx", "head"),
        P(),
        P("ctx", "head"),
        P("ctx", "head"),
        P("ctx", "head"),
        P("ctx", "head"),
    )
    return jax.shard_map(
        program,
        mesh=mesh,
        in_specs=placed,
        out_specs=(
            P("ctx", "head"),
            P("ctx", None),
            P("ctx", "head"),
            P("ctx", "head"),
            P(None, "head"),
            P("head"),
            P(),
            P(),
            P("head"),
            P("head"),
            P("head"),
            P("ctx", "head"),
            P("ctx", "head"),
            P("ctx", "head"),
        ),
        check_vma=False,
    )
```

```python
import math

import jax
import jax.numpy as jnp
from jax import lax
from jax.experimental import pallas as pl
from jax.experimental.pallas import tpu as pltpu
from jax.sharding import PartitionSpec as P


MP = 64
KC = 4
AH = 64
KVH = 8
HD = 128
RB = 128
FILL = -1e30
F32 = jnp.float32
BF16 = jnp.bfloat16
HIGHEST = lax.Precision.HIGHEST


def params(limit=56):
    return pltpu.CompilerParams(vmem_limit_bytes=limit * 1024 * 1024)


def shifted(value, axis, steps):
    count = lax.axis_size(axis)
    initial, last = (max(0, -steps), min(count, count - steps))
    return lax.ppermute(value, axis, [(source, source + steps) for source in range(initial, last)])


def crossed(value, axis, mask):
    count = lax.axis_size(axis)
    return lax.ppermute(value, axis, [(source, source ^ mask) for source in range(count)])


def dot(a, b, dims=((1,), (0,)), precision=None):
    return lax.dot_general(a, b, (dims, ((), ())), precision=precision, preferred_element_type=F32)


NN = ((1,), (0,))
NT = ((1,), (1,))
TN = ((0,), (0,))


def iota(shape, dim):
    return lax.broadcasted_iota(jnp.int32, shape, dim)


def doc_start(doc_ref, pos):
    end = jnp.int32(0)
    start = jnp.zeros_like(pos)
    for j in range(doc_ref.shape[0]):
        end = end + doc_ref[j]
        start = jnp.where(pos >= end, end, start)
    return start


def smem():
    return pl.BlockSpec(memory_space=pltpu.SMEM)


def vmem():
    return pl.BlockSpec(memory_space=pltpu.VMEM)


def attention_kernel(reach, idx_ref, doc_ref, q_ref, do_ref, *rest):
    nb = reach + 1
    kv_refs = rest[:nb]
    dq_ref = rest[nb]
    out_refs = rest[nb + 1 : 2 * nb + 1]
    k_ref, v_ref, kt_ref, mask_ref, qc_ref, dc_ref, p_ref, g_ref = rest[2 * nb + 1 :]
    group = AH // KVH
    kv_count = q_ref.shape[1] // (group * HD)
    inv_root = 1.0 / math.sqrt(HD)
    keys = nb * RB
    first = idx_ref[1] * RB
    q_pos = first + iota((8, RB), 1)
    q_start = doc_start(doc_ref, q_pos)[:1]
    k_pos = first - reach * RB + iota((keys, RB), 0)
    allowed = (k_pos <= q_pos[:1]) & (k_pos >= q_start)
    mask_ref[...] = jnp.where(allowed, 0.0, FILL)
    for kv in range(kv_count):
        for b in range(nb):
            k_ref[pl.ds(b * RB, RB), :] = kv_refs[b][:RB, pl.ds(kv * HD, HD)]
            v_ref[pl.ds(b * RB, RB), :] = kv_refs[b][:RB, pl.ds((kv_count + kv) * HD, HD)]
        kt_ref[...] = k_ref[...].astype(F32).T.astype(BF16)

        def one(h):
            lanes = pl.ds(pl.multiple_of((kv * group + h) * HD, HD), HD)
            rows = pl.ds(pl.multiple_of(h * RB, RB), RB)
            q = q_ref[:, lanes]
            do = do_ref[:, lanes]
            qc_ref[rows, :] = q
            dc_ref[rows, :] = do
            scores = dot(k_ref[...], q, NT) * inv_root + mask_ref[...]
            top = jnp.max(scores, axis=0, keepdims=True)
            weights = jnp.exp(scores - top)
            softmax = weights * (1.0 / jnp.sum(weights, axis=0, keepdims=True))
            grad_prob = dot(v_ref[...], do, NT)
            delta = jnp.sum(softmax * grad_prob, axis=0, keepdims=True)
            grad_score = (softmax * (grad_prob - delta)).astype(BF16)
            p_ref[:, rows] = softmax.astype(BF16)
            g_ref[:, rows] = grad_score
            grad_q = dot(kt_ref[...], grad_score, NN) * inv_root
            dq_ref[:, lanes] = grad_q.T.astype(BF16)

        def head(h, carry):
            one(2 * h)
            one(2 * h + 1)
            return carry

        lax.fori_loop(0, group // 2, head, 0)
        grad_k = dot(g_ref[...], qc_ref[...], NN) * inv_root
        grad_v = dot(p_ref[...], dc_ref[...], NN)
        for b in range(nb):
            kind = out_refs[b].dtype
            rows = slice(b * RB, (b + 1) * RB)
            out_refs[b][:, pl.ds(kv * HD, HD)] = grad_k[rows].astype(kind)
            out_refs[b][:, pl.ds((kv_count + kv) * HD, HD)] = grad_v[rows].astype(kind)


def attention_call(idx, doc, queries, grads, blocks):
    nb = len(blocks)
    keys = nb * RB
    group = AH // KVH
    outs = [jax.ShapeDtypeStruct(queries.shape, BF16)]
    outs += [jax.ShapeDtypeStruct(blocks[-1].shape, BF16)] * (nb - 1)
    outs += [jax.ShapeDtypeStruct(blocks[-1].shape, F32)]
    return pl.pallas_call(
        lambda *refs: attention_kernel(nb - 1, *refs),
        out_shape=outs,
        in_specs=[smem(), smem()] + [vmem()] * (2 + nb),
        out_specs=[vmem()] * (1 + nb),
        scratch_shapes=[
            pltpu.VMEM((keys, HD), BF16),
            pltpu.VMEM((keys, HD), BF16),
            pltpu.VMEM((HD, keys), BF16),
            pltpu.VMEM((keys, RB), F32),
            pltpu.VMEM((group * RB, HD), BF16),
            pltpu.VMEM((group * RB, HD), BF16),
            pltpu.VMEM((keys, group * RB), BF16),
            pltpu.VMEM((keys, group * RB), BF16),
        ],
        compiler_params=params(),
        name="attention",
    )(idx, doc, queries, grads, *blocks)


def pack_kernel(n, heads, idx_ref, x_ref, z_ref, d_ref, raw_ref, step_ref, *outs):
    half = heads * MP // 2
    me = idx_ref[0]
    lane = iota((x_ref.shape[0], 128), 1)
    for m in range(n):
        dest = me ^ m
        for side in range(2):
            out = outs[side * n + m]
            lanes = pl.ds(pl.multiple_of((2 * dest + side) * half, 128), half)
            z = z_ref[:, lanes].astype(F32)
            grad = d_ref[:, lanes].astype(F32) * z * jax.nn.sigmoid(z)
            out[:, :half] = x_ref[:, lanes]
            out[:, half : 2 * half] = grad.astype(BF16)
        outs[m][:, 2 * half : 2 * half + 256] = raw_ref[...]
        logit = pltpu.roll(step_ref[...], (128 - dest * heads) % 128, 1)
        high = logit.astype(BF16).astype(F32)
        middle = (logit - high).astype(BF16).astype(F32)
        rest = logit - high - middle
        parts = jnp.where(lane < heads, high, pltpu.roll(middle, heads, 1))
        parts = jnp.where(lane < 2 * heads, parts, pltpu.roll(rest, 2 * heads, 1))
        outs[m][:, 2 * half + 256 :] = parts.astype(BF16)


def pack_call(n, heads, idx, mixer_x, gate_z, d_mixer, raw, steps):
    rows = mixer_x.shape[0]
    return pl.pallas_call(
        lambda *refs: pack_kernel(n, heads, *refs),
        out_shape=[jax.ShapeDtypeStruct((rows, heads * MP + 384), BF16)] * n
        + [jax.ShapeDtypeStruct((rows, heads * MP), BF16)] * n,
        in_specs=[smem()] + [vmem()] * 5,
        out_specs=[vmem()] * (2 * n),
        compiler_params=params(),
        name="pack",
    )(idx, mixer_x, gate_z, d_mixer, raw, steps)


def keys_kernel(n, k_ref, v_ref, x_ref, raw_ref, own_ref, *outs):
    kv_width = k_ref.shape[1]
    width = x_ref.shape[1] // n
    half = width // 2
    own_ref[:, :kv_width] = k_ref[...]
    own_ref[:, kv_width:] = v_ref[...]
    for d in range(n):
        outs[d][:RB, :kv_width] = k_ref[...]
        outs[d][:RB, kv_width:] = v_ref[...]
        outs[d][RB : RB + 16, :] = x_ref[:, d * width : d * width + half]
        outs[d][RB + 16 : RB + 32, :] = x_ref[:, d * width + half : (d + 1) * width]
        outs[d][RB + 32 :, :256] = raw_ref[...]
        if 2 * kv_width > 256:
            outs[d][RB + 32 :, 256:] = jnp.zeros((16, 2 * kv_width - 256), BF16)


def keys_call(n, att_keys, att_values, mixer_x, mixer_bc):
    rows, kv_width = att_keys.shape
    last = rows // 16 - 1
    return pl.pallas_call(
        lambda *refs: keys_kernel(n, *refs),
        grid=(1,),
        out_shape=[jax.ShapeDtypeStruct((rows, 2 * kv_width), BF16)]
        + [jax.ShapeDtypeStruct((rows + 48, 2 * kv_width), BF16)] * n,
        in_specs=[
            pl.BlockSpec((rows, kv_width), lambda i: (0, 0)),
            pl.BlockSpec((rows, kv_width), lambda i: (0, 0)),
            pl.BlockSpec((16, mixer_x.shape[1]), lambda i: (last, 0)),
            pl.BlockSpec((16, 256), lambda i: (last, 0)),
        ],
        out_specs=[pl.BlockSpec((rows, 2 * kv_width), lambda i: (0, 0))]
        + [pl.BlockSpec((rows + 48, 2 * kv_width), lambda i: (0, 0))] * n,
        compiler_params=params(),
        name="keys",
    )(att_keys, att_values, mixer_x, mixer_bc)


def edges_kernel(n, hp, pairs, idx_ref, *refs):
    edges = refs[:n]
    logit_ref, margin_ref, share_ref, rows_ref = refs[n:]
    width = pairs * 128
    me = idx_ref[0]
    margin = jnp.zeros((16, 128), F32)
    total = jnp.zeros((16, 128), F32)
    first = hp + 8 * pairs + 16
    heads_at = first + 8 * pairs + 16
    for m in range(n):
        source = me ^ m
        held = pl.ds(pl.multiple_of(source * hp, 8), hp)
        rows_ref[0, held, :] = edges[m][:hp, :]
        for k in range(3):
            rows_ref[1 + k, held, :] = edges[m][heads_at + k * hp : heads_at + (k + 1) * hp, :]
        for p in range(pairs):
            part = pl.ds(pl.multiple_of(source * width + p * 128, 128), 128)
            margin_ref[:, part] = edges[m][hp + 8 * p : hp + 8 * p + 8, :]
            share_ref[:, part] = edges[m][first + 8 * p : first + 8 * p + 8, :]
        margin = margin + edges[m][hp + 8 * pairs : first, :]
        total = total + edges[m][first + 8 * pairs : heads_at, :]
    at = n * width
    margin_ref[:, at : at + 128] = margin[:8]
    margin_ref[:, at + 128 :] = margin[8:]
    share_ref[:, at : at + 128] = total[:8]
    share_ref[:, at + 128 : at + 256] = total[8:]
    ones = jnp.ones((8, 128), F32)
    for k in range(3):
        lanes = slice(at + 256 + k * n * hp, at + 256 + (k + 1) * n * hp)
        share_ref[:, lanes] = dot(ones, rows_ref[1 + k], NT, HIGHEST)
    logit_ref[...] = rows_ref[0].T


def edges_call(n, hp, pairs, idx, edges):
    return pl.pallas_call(
        lambda *refs: edges_kernel(n, hp, pairs, *refs),
        out_shape=[
            jax.ShapeDtypeStruct((RB, n * hp), F32),
            jax.ShapeDtypeStruct((8, n * pairs * 128 + 256), F32),
            jax.ShapeDtypeStruct((8, n * pairs * 128 + 256 + 3 * n * hp), F32),
        ],
        in_specs=[smem()] + [vmem()] * n,
        out_specs=[vmem()] * 3,
        scratch_shapes=[pltpu.VMEM((4, n * hp, 128), F32)],
        compiler_params=params(),
        name="edges",
    )(idx, *edges)


def unpack_kernel(n, hp, idx_ref, z_ref, d_ref, margin_ref, share_ref, *refs):
    gx_ref, gz_ref, taps_ref, bias_ref, heads_ref = refs[2 * n :]
    channels = z_ref.shape[1]
    width = channels // n // 2
    me = idx_ref[0]
    use = jnp.where(me == n - 1, 1.0, 0.0)
    for m in range(2 * n):
        piece = refs[m]
        lanes = pl.ds(pl.multiple_of((2 * (me ^ (m % n)) + m // n) * width, 128), width)
        gx_ref[: RB - 16, lanes] = piece[: RB - 16, :width]
        end = piece[RB - 16 :, :width].astype(F32)
        end = jnp.concatenate([end[:8], end[8:] + use * margin_ref[:, lanes]], axis=0)
        gx_ref[RB - 16 :, lanes] = end.astype(BF16)
        z = z_ref[:, lanes].astype(F32)
        sig = jax.nn.sigmoid(z)
        y = piece[:, width:].astype(F32)
        gz_ref[:, lanes] = (d_ref[:, lanes].astype(F32) * y * (sig * (1.0 + z * (1.0 - sig)))).astype(BF16)
    taps_ref[...] = share_ref[:KC, :channels]
    bias_ref[...] = share_ref[KC : KC + 1, :channels]
    for k in range(3):
        at = channels + 256 + k * n * hp
        heads_ref[k : k + 1, :] = share_ref[:1, at : at + n * hp]


def unpack_call(n, hp, idx, gate_z, d_mixer, margin, share, big):
    rows, channels = gate_z.shape
    return pl.pallas_call(
        lambda *refs: unpack_kernel(n, hp, *refs),
        out_shape=[
            jax.ShapeDtypeStruct((rows, channels), BF16),
            jax.ShapeDtypeStruct((rows, channels), BF16),
            jax.ShapeDtypeStruct((KC, channels), F32),
            jax.ShapeDtypeStruct((1, channels), F32),
            jax.ShapeDtypeStruct((3, n * hp), F32),
        ],
        in_specs=[smem()] + [vmem()] * (4 + 2 * n),
        out_specs=[vmem()] * 5,
        compiler_params=params(),
        name="unpack",
    )(idx, gate_z, d_mixer, margin, share, *big)


def by_sublane(value):
    return jnp.sum(value.reshape(value.shape[0] // 8, 8, value.shape[1]), axis=0)


class Shared:
    def __init__(self, n, heads, side, idx_ref, doc_ref, ins, scratch, full):
        self.n = n
        self.me = me = idx_ref[0]
        first = (idx_ref[1] - me) * RB
        xd_in = ins[:n]
        tails = ins[n : 2 * n]
        aux = ins[2 * n : 3 * n] if side else xd_in
        self.wx_ref, self.bx_ref, wbc_ref, bbc_ref, par_ref = ins[-5:]
        self.par_ref = par_ref
        self.side = side
        self.width = width = heads * MP
        self.tail_ref, self.xd_ref, self.raw_ref, self.off_ref, self.xs_ref = scratch[:5]
        self.bb_ref, self.cc_ref, self.bt_ref, self.ct_ref, self.step_ref, self.cum_ref = scratch[5:11]
        if full:
            self.cb_ref, self.bias_ref, self.sg_ref = scratch[11:14]
        self.lane = lane = iota((RB, 128), 1)
        self.sub = sub = iota((RB, 128), 0)
        self.low = lane < MP
        upper = (sub <= lane).astype(F32)
        self.e_log = e_log = jnp.exp(par_ref[0])
        for m in range(n):
            source = me ^ m
            self.tail_ref[m, :, :width] = tails[m][RB + 16 * side : RB + 16 * side + 16, :]
            self.tail_ref[m, :, width:] = tails[m][RB + 32 : RB + 48, :256]
            self.xd_ref[self.rows(source), :] = xd_in[m][:, : 2 * width]
            raw = aux[m][:, 2 * width : 2 * width + 256]
            self.raw_ref[pl.ds(pl.multiple_of(source * RB + 8, 8), RB), :] = raw.astype(F32)
            parts = aux[m][:, 2 * width + 256 :].astype(F32).T
            at = side * heads
            logit = parts[at : at + heads] + parts[at + 2 * heads : at + 3 * heads] + parts[at + 4 * heads : at + 5 * heads]
            logit = logit + par_ref[1]
            step = jnp.maximum(logit, 0.0) + jnp.log1p(jnp.exp(-jnp.abs(logit)))
            self.step_ref[source] = step
            if full:
                self.sg_ref[source] = jax.nn.sigmoid(logit)
            self.cum_ref[source] = dot(-step * e_log, upper, NN, HIGHEST)
        self.raw_ref[:8, :] = self.tail_ref[me, :, width:].astype(F32)[8:]
        self.wbc = wbc = wbc_ref[...]
        self.bbc = bbc = bbc_ref[...]

        def prepare(c, carry):
            pos = first + c * RB + sub
            off = pos - doc_start(doc_ref, pos)
            self.off_ref[self.rows(c), :] = off
            masks = [off >= j for j in range(KC)]
            pre_b = self.conv(c, self.raw_ref, slice(0, 128), wbc[:, :128], bbc[:, :128], masks)
            pre_c = self.conv(c, self.raw_ref, slice(128, 256), wbc[:, 128:], bbc[:, 128:], masks)
            b_in = pre_b * jax.nn.sigmoid(pre_b)
            c_out = pre_c * jax.nn.sigmoid(pre_c)
            self.bt_ref[c] = b_in.T.astype(BF16)
            self.ct_ref[c] = c_out.T.astype(BF16)
            if full:
                allowed = (lane <= sub) & (sub - lane <= off)
                self.bias_ref[c] = jnp.where(allowed, 0.0, FILL)
                b_low, c_low = b_in.astype(BF16), c_out.astype(BF16)
                self.bb_ref[self.rows(c), :] = b_low
                self.cc_ref[self.rows(c), :] = c_low
                self.cb_ref[c] = dot(c_low, b_low, NT)
            return carry

        lax.fori_loop(0, n, prepare, 0)

    def rows(self, c, extra=0):
        return pl.ds(pl.multiple_of(c * RB, RB), RB + extra)

    def conv(self, c, src_ref, lanes, weight, bias, masks):
        window = src_ref[self.rows(c, 8), lanes]
        pre = bias + weight[0:1] * window[8:]
        for j in range(1, KC):
            pre = pre + weight[j : j + 1] * jnp.where(masks[j], window[8 - j : 8 + RB - j], 0.0)
        return pre

    def masks(self, c):
        off = self.off_ref[self.rows(c), :]
        return off, [off >= j for j in range(KC)]

    def load(self, u, lanes):
        self.xs_ref[u, :8, :] = self.tail_ref[self.me, :, lanes].astype(F32)[8:]

        def one(c, unused):
            rows = pl.ds(pl.multiple_of(c * RB + 8, 8), RB)
            self.xs_ref[u, rows, :] = self.xd_ref[self.rows(c), lanes].astype(F32)
            return unused

        lax.fori_loop(0, self.n, one, 0)

    def decays(self, last_off, off, cum):
        last = cum[RB - 1 :]
        enter = jnp.where(off > self.sub, jnp.exp(cum), 0.0)
        leave = jnp.where(self.sub >= RB - 1 - last_off, jnp.exp(last - cum), 0.0)
        keep = jnp.where(last_off >= RB, jnp.exp(last), 0.0)
        return enter, leave, keep

    def held(self, p):
        return pl.ds(pl.multiple_of((2 * self.me + self.side) * self.width + p * 128, 128), 128)

    def pair_rows(self, ref, c, p):
        return ref[c, pl.ds(2 * p, 1), :], ref[c, pl.ds(2 * p + 1, 1), :]


def shared_scratch(n, heads, wide, full):
    width = heads * MP
    tokens = n * RB
    found = [
        pltpu.VMEM((n, 16, width + 256), BF16),
        pltpu.VMEM((tokens, 2 * width), BF16),
        pltpu.VMEM((tokens + 8, 256), F32),
        pltpu.VMEM((tokens, 128), jnp.int32),
        pltpu.VMEM((wide, tokens + 8, 128), F32),
        pltpu.VMEM((tokens, 128), BF16),
        pltpu.VMEM((tokens, 128), BF16),
        pltpu.VMEM((n, 128, RB), BF16),
        pltpu.VMEM((n, 128, RB), BF16),
        pltpu.VMEM((n, heads, 128), F32),
        pltpu.VMEM((n, heads, 128), F32),
    ]
    if full:
        found += [
            pltpu.VMEM((n, RB, RB), F32),
            pltpu.VMEM((n, RB, RB), F32),
            pltpu.VMEM((n, heads, 128), F32),
        ]
    return found


def totals_kernel(n, heads, side, wide, idx_ref, doc_ref, *refs):
    pairs = heads * MP // 128
    width = heads * MP
    at = (2 + side) * n + 5
    ins = refs[:at]
    state_ref, grad_ref, keep_ref = refs[at : at + 3]
    sh = Shared(n, heads, side, idx_ref, doc_ref, ins, refs[at + 3 :], False)

    def streams(block, carry):
        ids = [block * wide + u for u in range(wide)]
        held = [sh.held(p) for p in ids]
        weight = [sh.wx_ref[:, h] for h in held]
        bias = [sh.bx_ref[:, h] for h in held]
        for u in range(wide):
            sh.load(u, pl.ds(pl.multiple_of(ids[u] * 128, 128), 128))

        def one(u, c, off, masks, state, grads, kept):
            p = ids[u]
            pre = sh.conv(c, sh.xs_ref.at[u], slice(None), weight[u], bias[u], masks)
            x = pre * jax.nn.sigmoid(pre)
            row0, row1 = sh.pair_rows(sh.cum_ref, c, p)
            step0, step1 = sh.pair_rows(sh.step_ref, c, p)
            cum = jnp.where(sh.sub < MP, row0, row1).T
            step = jnp.where(sh.sub < MP, step0, step1).T
            enter, leave, keep = sh.decays(off[RB - 1 :], off, cum)
            grad = sh.xd_ref[sh.rows(c), pl.ds(pl.multiple_of(width + p * 128, 128), 128)].astype(F32)
            state = keep * state + dot(sh.bt_ref[c], (leave * (step * x)).astype(BF16), NN)
            grads = grads + kept * dot(sh.ct_ref[c], (enter * grad).astype(BF16), NN)
            return state, grads, kept * keep

        def chunk(c, held):
            off, masks = sh.masks(c)
            return tuple(one(u, c, off, masks, *held[u]) for u in range(wide))

        zero = jnp.zeros((128, 128), F32)
        found = lax.fori_loop(0, n, chunk, tuple((zero, zero, jnp.ones((1, 128), F32)) for _ in range(wide)))
        for u in range(wide):
            state_ref[ids[u]] = found[u][0].astype(BF16)
            grad_ref[ids[u]] = found[u][1].astype(BF16)
            keep_ref[ids[u]] = jnp.broadcast_to(found[u][2], (8, 128))
        return carry

    lax.fori_loop(0, pairs // wide, streams, 0)


def totals_call(n, heads, side, idx, doc, ins):
    pairs = heads * MP // 128
    wide = 2 - pairs % 2
    return pl.pallas_call(
        lambda *refs: totals_kernel(n, heads, side, wide, *refs),
        out_shape=[
            jax.ShapeDtypeStruct((pairs, 128, 128), BF16),
            jax.ShapeDtypeStruct((pairs, 128, 128), BF16),
            jax.ShapeDtypeStruct((pairs, 8, 128), F32),
        ],
        in_specs=[smem(), smem()] + [vmem()] * len(ins),
        out_specs=[vmem()] * 3,
        scratch_shapes=shared_scratch(n, heads, wide, False),
        compiler_params=params(),
    )(idx, doc, *ins)


def mixer_kernel(n, heads, side, wide, idx_ref, doc_ref, *refs):
    width = heads * MP
    pairs = width // 128
    all_rows = 2 * heads
    at = (2 + side) * n + 5
    ins = refs[:at]
    first_ref, later_ref = refs[at : at + 2]
    at = at + 2
    if side:
        sums_in = refs[at : at + 3]
        logit_in, part_in = refs[at + 3 : at + 5]
        at = at + 5
    big_out = refs[at : at + n]
    at = at + n
    if side:
        bc_out = refs[at : at + n]
        edge_out = refs[at + n : at + 2 * n]
        dcb_ref, db_ref, dc_ref, og_ref = refs[at + 2 * n : at + 2 * n + 4]
        at = at + 2 * n + 4
    else:
        dcb_ref, db_ref, dc_ref, logit_out, part_out = refs[at : at + 5]
        at = at + 5
    (
        od_ref,
        gp_ref,
        z1_ref,
        z2_ref,
        sin_ref,
        yn_ref,
        dwi_ref,
        lv_ref,
        st_ref,
        xc_ref,
        ds_ref,
        ed_ref,
        k_ref,
        acc_ref,
        skip_ref,
    ) = refs[at : at + 15]
    sh = Shared(n, heads, side, idx_ref, doc_ref, ins, refs[at + 15 :], True)
    hp = heads
    me, lane, sub, low = sh.me, sh.lane, sh.sub, sh.low
    par_ref, wx_ref, bx_ref, xd_ref = sh.par_ref, sh.wx_ref, sh.bx_ref, sh.xd_ref
    raw_ref, xs_ref, cum_ref, step_ref = sh.raw_ref, sh.xs_ref, sh.cum_ref, sh.step_ref
    bb_ref, cc_ref, bt_ref, ct_ref = sh.bb_ref, sh.cc_ref, sh.bt_ref, sh.ct_ref
    cb_ref, bias_ref, sg_ref = sh.cb_ref, sh.bias_ref, sh.sg_ref
    wbc, bbc, e_log, conv, rows_of = sh.wbc, sh.bbc, sh.e_log, sh.conv, sh.rows
    tokens = n * RB
    sums_at = all_rows + 16 * pairs + 16
    zero8 = jnp.zeros((8, 128), F32)
    for c in range(n):
        z1_ref[c] = jnp.zeros((hp, 128), F32)
        z2_ref[c] = jnp.zeros((hp, 128), F32)
        for held_ref, k in ((dcb_ref, 0), (db_ref, 1), (dc_ref, 2)):
            held_ref[c] = sums_in[k][c] if side else jnp.zeros((RB, RB), F32)
    skip_ref[...] = jnp.zeros((hp, 128), F32)
    for u in range(wide):
        for j in range(KC - 1):
            gp_ref[u, j, tokens:, :] = zero8

    def conv_back(c, grad, src_ref, lanes, weight, u, masks):
        window = src_ref[rows_of(c, 8), lanes]
        back = weight[0:1] * grad
        sums = [by_sublane(grad * window[8:])]
        for j in range(1, KC):
            held_back = jnp.where(masks[j], grad, 0.0)
            sums.append(by_sublane(held_back * window[8 - j : 8 + RB - j]))
            gp_ref[u, j - 1, rows_of(c), :] = held_back
            back = back + weight[j : j + 1] * gp_ref[u, j - 1, rows_of(c, 8), :][j : j + RB]
        sums.append(by_sublane(grad))
        return back, sums

    def silu_parts(pre):
        sig = jax.nn.sigmoid(pre)
        return pre * sig, sig * (1.0 + pre * (1.0 - sig))

    def margin_of(weight, u):
        total = zero8
        for j in range(1, KC):
            turned = pltpu.roll(gp_ref[u, j - 1, :8, :], 8 - j, 0)
            total = total + weight[j : j + 1] * jnp.where(sub[:8] >= 8 - j, turned, 0.0)
        return total

    def streams(block, carry):
        ids = [block * wide + u for u in range(wide)]
        each = range(wide)
        lanes = [pl.ds(pl.multiple_of(p * 128, 128), 128) for p in ids]
        lanes_d = [pl.ds(pl.multiple_of(width + p * 128, 128), 128) for p in ids]
        held = [sh.held(p) for p in ids]
        weight = [wx_ref[:, h] for h in held]
        bias = [bx_ref[:, h] for h in held]
        skip = [
            jnp.where(low[:1], par_ref[2, pl.ds(2 * p, 1), :], par_ref[2, pl.ds(2 * p + 1, 1), :]) for p in ids
        ]
        pick = [
            jnp.where(iota((hp, 128), 0) == 2 * p + iota((hp, 128), 1) // MP, 1.0, 0.0).astype(BF16) for p in ids
        ]

        for u in each:
            sh.load(u, lanes[u])

        def forward_one(u, c, off, masks, state):
            p = ids[u]
            rows = rows_of(c)
            pre = conv(c, xs_ref.at[u], slice(None), weight[u], bias[u], masks)
            x, slope = silu_parts(pre)
            xc_ref[u, rows, :] = x
            ds_ref[u, rows, :] = slope
            row0 = cum_ref[c, pl.ds(2 * p, 1), :]
            row1 = cum_ref[c, pl.ds(2 * p + 1, 1), :]
            col0 = jnp.broadcast_to(row0, (128, RB)).T
            col1 = jnp.broadcast_to(row1, (128, RB)).T
            step0 = step_ref[c, pl.ds(2 * p, 1), :]
            step1 = step_ref[c, pl.ds(2 * p + 1, 1), :]
            step = jnp.where(sub < MP, step0, step1).T
            st_ref[u, rows, :] = step
            cum = jnp.where(low, col0, col1)
            mask = bias_ref[c]
            cb = cb_ref[c]
            decay0 = jnp.exp(col0 - row0 + mask)
            decay1 = jnp.exp(col1 - row1 + mask)
            mix0 = (decay0 * cb).astype(BF16)
            mix1 = (decay1 * cb).astype(BF16)
            value = step * x
            grad = xd_ref[rows, lanes_d[u]].astype(F32)
            value_low = value.astype(BF16)
            value_two = jnp.concatenate(
                [jnp.where(low, value, 0.0).astype(BF16), jnp.where(low, 0.0, value).astype(BF16)], axis=0
            )
            grad_two = jnp.concatenate(
                [jnp.where(low, grad, 0.0).astype(BF16), jnp.where(low, 0.0, grad).astype(BF16)], axis=0
            )
            inner = dot(jnp.concatenate([mix0, mix1], axis=1), value_two, NN)
            dwi_ref[u, rows, :] = dot(jnp.concatenate([mix0, mix1], axis=0), grad_two, TN)
            grad_mix = dot(grad_two, value_low, NT)
            added = decay0 * grad_mix[:RB] + decay1 * grad_mix[RB:]
            enter, leave, keep = sh.decays(off[RB - 1 :], off, cum)
            lv_ref[u, rows, :] = leave
            k_ref[u, c] = jnp.broadcast_to(keep, (8, 128))
            sin_ref[u, c] = state
            state_low = state.astype(BF16)
            total = inner + enter * dot(cc_ref[rows, :], state_low, NN)
            yn_ref[u, rows, :] = total
            od_ref[rows, lanes_d[u]] = (total + skip[u] * x).astype(BF16)
            entered = (enter * grad).astype(BF16)
            ed_ref[u, rows, :] = entered
            new_state = keep * state + dot(bt_ref[c], (leave * value).astype(BF16), NN)
            return new_state, added, dot(entered, state_low, NT)

        def forward(c, states):
            off, masks = sh.masks(c)
            found = [forward_one(u, c, off, masks, states[u]) for u in each]
            dcb_ref[c] += sum(f[1] for f in found)
            dc_ref[c] += sum(f[2] for f in found)
            return tuple(f[0] for f in found)

        final = lax.fori_loop(0, n, forward, tuple(first_ref[p].astype(F32) for p in ids))
        for u in each:
            sin_ref[u, n] = final[u]
            for j in range(KC + 2):
                acc_ref[u, j] = zero8

        def backward_one(u, c, masks, later):
            rows = rows_of(c)
            later_low = later.astype(BF16)
            leave = lv_ref[u, rows, :]
            x = xc_ref[u, rows, :]
            step = st_ref[u, rows, :]
            grad = xd_ref[rows, lanes_d[u]].astype(F32)
            value = step * x
            grad_value = dwi_ref[u, rows, :] + leave * dot(bb_ref[rows, :], later_low, NN)
            z1 = grad * yn_ref[u, rows, :] - value.astype(BF16).astype(F32) * grad_value
            carried = jnp.sum(later_low.astype(F32) * sin_ref[u, c + 1], axis=0, keepdims=True)
            z1 = jnp.concatenate([z1[: RB - 8], z1[RB - 8 :] + jnp.where(sub[RB - 8 :] == RB - 1, carried, 0.0)], axis=0)
            z1_high = z1.astype(BF16)
            z1_rest = (z1 - z1_high.astype(F32)).astype(BF16)
            rates = dot(pick[u], z1_high, NT) + dot(pick[u], z1_rest, NT)
            steps = dot(pick[u], (x * grad_value).astype(BF16), NT)
            grad_b = dot((leave * value).astype(BF16), later_low, NT)
            grad_x = (step * grad_value + skip[u] * grad) * ds_ref[u, rows, :]
            back, sums = conv_back(c, grad_x, xs_ref.at[u], slice(None), weight[u], u, masks)
            od_ref[rows, lanes[u]] = back.astype(BF16)
            sums.append(by_sublane(grad * x))
            for j in range(KC + 2):
                acc_ref[u, j] += sums[j]
            new_later = k_ref[u, c][:1] * later + dot(ct_ref[c], ed_ref[u, rows, :], NN)
            return new_later, rates, steps, grad_b

        def backward(k, laters):
            c = n - 1 - k
            _, masks = sh.masks(c)
            found = [backward_one(u, c, masks, laters[u]) for u in each]
            z1_ref[c] += sum(f[1] for f in found)
            z2_ref[c] += sum(f[2] for f in found)
            db_ref[c] += sum(f[3] for f in found)
            return tuple(f[0] for f in found)

        lax.fori_loop(0, n, backward, tuple(later_ref[p].astype(F32) for p in ids))
        for u in each:
            found = [jnp.sum(acc_ref[u, j], axis=0, keepdims=True) for j in range(KC + 2)]
            skip_ref[...] += pick[u].astype(F32) * found[KC + 1]
            found = found[: KC + 1] + [jnp.zeros((8 - KC - 1, 128), F32)]
            if side:
                taps_to, taps_at = edge_out[0], sums_at + 8 * (pairs + ids[u])
                margin_to, margin_at = edge_out[0], all_rows + 8 * (pairs + ids[u])
            else:
                taps_to, taps_at = part_out, 8 * (pairs + ids[u])
                margin_to, margin_at = part_out, 8 * ids[u]
            taps_to[pl.ds(pl.multiple_of(taps_at, 8), 8), :] = jnp.concatenate(found, axis=0)
            margin_to[pl.ds(pl.multiple_of(margin_at, 8), 8), :] = margin_of(weight[u], u)
        return carry

    lax.fori_loop(0, pairs // wide, streams, 0)

    for part in range(2 if side else 0):
        lanes = slice(128 * part, 128 * part + 128)
        weight = wbc[:, lanes]
        bias = bbc[:, lanes]
        for j in range(KC + 1):
            acc_ref[0, j] = zero8

        def finish(k, carry):
            c = n - 1 - k
            rows = rows_of(c)
            mixed = dcb_ref[c].astype(BF16)
            if part == 0:
                grad = db_ref[c] + dot(mixed, cc_ref[rows, :], TN)
            else:
                grad = dc_ref[c] + dot(mixed, bb_ref[rows, :], NN)
            _, masks = sh.masks(c)
            pre = conv(c, raw_ref, lanes, weight, bias, masks)
            back, sums = conv_back(c, grad * silu_parts(pre)[1], raw_ref, lanes, weight, 0, masks)
            og_ref[rows, lanes] = back.astype(BF16)
            for j in range(KC + 1):
                acc_ref[0, j] += sums[j]
            return carry

        lax.fori_loop(0, n, finish, 0)
        found = [jnp.sum(acc_ref[0, j], axis=0, keepdims=True) for j in range(KC + 1)]
        found.append(jnp.zeros((8 - KC - 1, 128), F32))
        at_row = 16 * pairs + 8 * part
        edge_out[0][sums_at + at_row : sums_at + at_row + 8, :] = jnp.concatenate(found, axis=0)
        edge_out[0][all_rows + at_row : all_rows + at_row + 8, :] = margin_of(weight, 0)

    later_sum = (sub >= lane).astype(F32)
    sum_log = jnp.zeros((hp, 128), F32)
    sum_step = jnp.zeros((hp, 128), F32)
    for m in range(n):
        c = me ^ m
        rate_grad = dot(z1_ref[c], later_sum, NN, HIGHEST)
        step_grad = z2_ref[c] - e_log * rate_grad
        logit_grad = step_grad * sg_ref[c]
        sum_log = sum_log - step_ref[c] * e_log * rate_grad
        sum_step = sum_step + logit_grad
        if side:
            edge_out[m][:hp, :] = logit_in[c]
            edge_out[m][hp:all_rows, :] = logit_grad
            bc_out[m][...] = og_ref[rows_of(c), :]
        else:
            logit_out[c] = logit_grad
        big_out[m][...] = od_ref[rows_of(c), :]
    if side:
        edge_out[0][all_rows : all_rows + 8 * pairs, :] = part_in[: 8 * pairs, :]
        edge_out[0][sums_at : sums_at + 8 * pairs, :] = part_in[8 * pairs : 16 * pairs, :]
    for k, value in enumerate((sum_log, sum_step, skip_ref[...])):
        if side:
            at_row = sums_at + 16 * pairs + 16 + k * all_rows
            edge_out[0][at_row : at_row + hp, :] = part_in[16 * pairs + k * hp : 16 * pairs + (k + 1) * hp, :]
            edge_out[0][at_row + hp : at_row + all_rows, :] = value
        else:
            part_out[16 * pairs + k * hp : 16 * pairs + (k + 1) * hp, :] = value
    for m in range(1, n if side else 0):
        edge_out[m][all_rows:, :] = edge_out[0][all_rows:, :]


def mixer_call(n, heads, side, idx, doc, ins, first, later, earlier):
    width = heads * MP
    pairs = width // 128
    wide = 2 - pairs % 2
    tokens = n * RB
    square = jax.ShapeDtypeStruct((n, RB, RB), F32)
    flat = pltpu.VMEM((wide, tokens, 128), F32)
    per_head = pltpu.VMEM((n, heads, 128), F32)
    outs = [jax.ShapeDtypeStruct((RB, 2 * width), BF16)] * n
    if side:
        outs += [jax.ShapeDtypeStruct((RB, 256), BF16)] * n
        outs += [jax.ShapeDtypeStruct((8 * heads + 32 * pairs + 32, 128), F32)] * n
        sums = [pltpu.VMEM((n, RB, RB), F32)] * 3 + [pltpu.VMEM((tokens, 256), BF16)]
    else:
        outs += [square] * 3
        outs += [jax.ShapeDtypeStruct((n, heads, 128), F32)]
        outs += [jax.ShapeDtypeStruct((16 * pairs + 3 * heads, 128), F32)]
        sums = []
    return pl.pallas_call(
        lambda *refs: mixer_kernel(n, heads, side, wide, *refs),
        out_shape=outs,
        in_specs=[smem(), smem()] + [vmem()] * (len(ins) + 2 + len(earlier)),
        out_specs=[vmem()] * len(outs),
        scratch_shapes=sums
        + [
            pltpu.VMEM((tokens, 2 * width), BF16),
            pltpu.VMEM((wide, KC - 1, tokens + 8, 128), F32),
            per_head,
            per_head,
            pltpu.VMEM((wide, n + 1, 128, 128), F32),
            flat,
            flat,
            flat,
            flat,
            flat,
            flat,
            pltpu.VMEM((wide, tokens, 128), BF16),
            pltpu.VMEM((wide, n, 8, 128), F32),
            pltpu.VMEM((wide, KC + 2, 8, 128), F32),
            pltpu.VMEM((heads, 128), F32),
        ]
        + shared_scratch(n, heads, wide, True),
        compiler_params=params(),
    )(idx, doc, *ins, first, later, *earlier)


def program(
    mixer_x,
    mixer_bc,
    dt_raw,
    gate_z,
    conv_weight_x,
    conv_bias_x,
    conv_weight_bc,
    conv_bias_bc,
    a_log,
    dt_bias,
    skip_d,
    d_mixer,
    doc_lengths,
    att_queries,
    att_keys,
    att_values,
    d_attn,
):
    n = lax.axis_size("ctx")
    group = min(4, n)
    place = lax.axis_index("ctx")
    inside = place % group
    idx = jnp.stack([inside, place]).astype(jnp.int32)
    rows, channels = mixer_x.shape
    all_heads = channels // MP
    heads = all_heads // group
    hp = heads
    width = heads * MP
    pairs = width // 128
    reach = max(1, n // 2)

    sent = keys_call(group, att_keys, att_values, mixer_x, mixer_bc)
    own = sent[0]
    reached = [shifted(sent[d] if d <= group else own, "ctx", d) for d in range(1, max(reach, group) + 1)]
    tails = reached[:group]
    blocks = reached[:reach][::-1] + [own]

    logits = jnp.pad(dt_raw, ((0, 0), (0, 128 - all_heads)))
    packed = pack_call(group, heads, idx, mixer_x, gate_z, d_mixer, mixer_bc, logits)
    big = []
    for side in range(2):
        piece = packed[side * group : (side + 1) * group]
        big.append([piece[0]] + [crossed(piece[m], "ctx", m) for m in range(1, group)])

    half = heads // 2
    head_params = jnp.stack([a_log, dt_bias, skip_d])
    head_params = lax.dynamic_slice_in_dim(head_params, inside * heads, heads, 1)
    head_params = jnp.broadcast_to(head_params[:, :, None], (3, heads, 128))
    ins = []
    entering = []
    for side in range(2):
        ins.append(
            big[side]
            + tails
            + (big[0] if side else [])
            + [conv_weight_x, conv_bias_x[None], conv_weight_bc, conv_bias_bc[None]]
            + [head_params[:, side * half : (side + 1) * half]]
        )
        state, back_state, keep = totals_call(group, half, side, idx, doc_lengths, ins[side])
        back_keep = keep
        covered = 1
        while covered < n // group // 2:
            step_by = covered * group
            state = (state.astype(F32) + keep[:, :1] * shifted(state, "ctx", step_by).astype(F32)).astype(BF16)
            back_state = (
                back_state.astype(F32) + back_keep[:, :1] * shifted(back_state, "ctx", -step_by).astype(F32)
            ).astype(BF16)
            keep = keep * shifted(keep, "ctx", step_by)
            back_keep = back_keep * shifted(back_keep, "ctx", -step_by)
            covered = 2 * covered
        entering.append((shifted(state, "ctx", group), shifted(back_state, "ctx", -group)))

    attended = attention_call(idx, doc_lengths, att_queries, d_attn, blocks)
    grad_queries = attended[0]
    grad_kv = attended[-1]
    arrived = [shifted(attended[1 + reach - d], "ctx", -d) for d in range(1, reach + 1)]
    for part in arrived:
        grad_kv = grad_kv + part.astype(F32)
    kv_width = att_keys.shape[1]
    grad_keys = grad_kv[:, :kv_width].astype(BF16)
    grad_values = grad_kv[:, kv_width:].astype(BF16)

    first = mixer_call(group, half, 0, idx, doc_lengths, ins[0], *entering[0], [])
    big = [first[0]] + [crossed(first[m], "ctx", m) for m in range(1, group)]
    results = mixer_call(group, half, 1, idx, doc_lengths, ins[1], *entering[1], first[group:])
    edges = [results[2 * group]] + [crossed(results[2 * group + m], "ctx", m) for m in range(1, group)]
    bc_parts = [results[group]] + [crossed(results[group + m], "ctx", m) for m in range(1, group)]
    big = big + [results[0]] + [crossed(results[m], "ctx", m) for m in range(1, group)]

    grad_logits, margin, share = edges_call(group, hp, pairs, idx, edges)
    margin = shifted(margin, "ctx", -1)
    mask = group
    while mask < n:
        share = share + crossed(share, "ctx", mask)
        mask = 2 * mask

    bc_sum = bc_parts[0].astype(F32)
    for m in range(1, group):
        bc_sum = bc_sum + bc_parts[m].astype(F32)
    bc_margin = jnp.where(inside == group - 1, margin[:, channels:], 0.0)
    bc_sum = jnp.concatenate([bc_sum[: rows - 8], bc_sum[rows - 8 :] + bc_margin], axis=0)
    both = jnp.concatenate([bc_sum, share[:, channels : channels + 256]], axis=0)
    total = both
    for m in range(1, lax.axis_size("head")):
        total = total + crossed(both, "head", m)
    grad_bc = total[:rows].astype(BF16)
    grad_weight_bc = total[rows : rows + KC]
    grad_bias_bc = total[rows + KC]

    grad_x, grad_z, taps, bias_sum, head_sums = unpack_call(group, hp, idx, gate_z, d_mixer, margin, share, big)
    return (
        grad_x,
        grad_bc,
        grad_logits,
        grad_z,
        taps,
        bias_sum[0],
        grad_weight_bc,
        grad_bias_bc,
        head_sums[0],
        head_sums[1],
        head_sums[2],
        grad_queries,
        grad_keys,
        grad_values,
    )


def solution(mesh):
    placed = (
        P("ctx", "head"),
        P("ctx", None),
        P("ctx", "head"),
        P("ctx", "head"),
        P(None, "head"),
        P("head"),
        P(),
        P(),
        P("head"),
        P("head"),
        P("head"),
        P("ctx", "head"),
        P(),
        P("ctx", "head"),
        P("ctx", "head"),
        P("ctx", "head"),
        P("ctx", "head"),
    )
    return jax.shard_map(
        program,
        mesh=mesh,
        in_specs=placed,
        out_specs=(
            P("ctx", "head"),
            P("ctx", None),
            P("ctx", "head"),
            P("ctx", "head"),
            P(None, "head"),
            P("head"),
            P(),
            P(),
            P("head"),
            P("head"),
            P("head"),
            P("ctx", "head"),
            P("ctx", "head"),
            P("ctx", "head"),
        ),
        check_vma=False,
    )
```
